32 devices in a mesh: batch: 8 (over y, x, core), seq: 4 (over z).
Axes of the slice: x: 2, y: 2, z: 4, core: 2. Of those that a mesh axis runs over, the one named last changes fastest.
Arguments:
- activations: float32 [8, 512, 960], P('batch', 'seq'), may hold values from -8 to 8
- segment_ids: int32 [8, 512], P('batch', 'seq'), may hold values from 0 to 2, never falling along the last dimension, each value on 1 to 384 neighbouring positions
- attention_gain: float32 [960], replicated, may hold values from 0.5 to 1.5
- query_weight: bfloat16 [960, 960], P('batch', 'seq'), may hold values from -0.117657917 to 0.117657917
- key_weight: bfloat16 [960, 320], P('batch', 'seq'), may hold values from -0.117657917 to 0.117657917
- value_weight: bfloat16 [960, 320], P('batch', 'seq'), may hold values from -0.1875 to 0.1875
- output_weight: bfloat16 [960, 960], P('batch', 'seq'), may hold values from -0.75 to 0.75
- feed_gain: float32 [960], replicated, may hold values from 0.5 to 1.5
- gate_weight: bfloat16 [960, 2560], P('batch', 'seq'), may hold values from -0.1875 to 0.1875
- up_weight: bfloat16 [960, 2560], P('batch', 'seq'), may hold values from -0.1875 to 0.1875
- down_weight: bfloat16 [2560, 960], P('seq', 'batch'), may hold values from -0.125 to 0.125
- out_grad: float32 [8, 512, 960], P('batch', 'seq'), may hold values from -6 to 6
Outputs:
- block_output: float32 [8, 512, 960], P('batch', 'seq')
- input_grad: float32 [8, 512, 960], P('batch', 'seq')
- attention_gain_grad: float32 [960], replicated
- query_weight_grad: float32 [960, 960], P('batch', 'seq')
- key_weight_grad: float32 [960, 320], P('batch', 'seq')
- value_weight_grad: float32 [960, 320], P('batch', 'seq')
- output_weight_grad: float32 [960, 960], P('batch', 'seq')
- feed_gain_grad: float32 [960], replicated
- gate_weight_grad: float32 [960, 2560], P('batch', 'seq')
- up_weight_grad: float32 [960, 2560], P('batch', 'seq')
- down_weight_grad: float32 [2560, 960], P('seq', 'batch')
The draws below stay inside these ranges and needn't reach their ends.
All inputs are finite; a program needn't handle non-finite values.
Results may differ from the reference program's by a relative error of at most 0.014.
The reference program's roundings to bfloat16 on the way count: a program that leaves them out, or rounds other values in their place, can miss the bound.
Values may be sent and summed in bfloat16 or wider, within the bound.
No kernel may reach another device: no remote copies, remote signals or barrier semaphores. Data moves between devices by JAX's collectives and lax.ppermute only.
A program may use at most 128 MiB of HBM per device.

```python
import math
import jax
import jax.numpy as jnp
import numpy as np
from jax import lax

D = 960
HEADS = 15
KV_HEADS = 5
HEAD_DIM = 64
FF = 2560
KVW = 320
LENGTH = 512
SEQS = 8


def projection(key, width, salt):
    base_key = jax.random.fold_in(key, salt)
    drawn = jax.random.truncated_normal(base_key, -3.0, 3.0, (D, width), jnp.float32) * D ** (-0.5)
    return drawn.astype(jnp.bfloat16)


def draw_query_weight(key, part):
    return projection(key, D, 11)


def draw_key_weight(key, part):
    return projection(key, KV_HEADS * HEAD_DIM, 12)


def draw_activations(key, part):
    shape = (SEQS, LENGTH, D)
    noise_key = jax.random.fold_in(key, 21)
    return jax.random.truncated_normal(noise_key, -6.0, 6.0, shape, jnp.float32)


def block_levels(key, extent, split, least, high):
    level = 1.0
    for axis_at, blocks in split:
        heights = jax.random.uniform(jax.random.fold_in(jax.random.fold_in(key, 6), axis_at), (blocks,), jnp.float32, least / len(split), high / len(split))
        level = level * jnp.repeat(jnp.exp(heights), extent[axis_at] // blocks).reshape((-1,) + (1,) * (len(extent) - 1 - axis_at))
    return level


def length_profile(count, total, most, lean):
    portions = [(1 << 20) // math.isqrt(rank ** lean) + 1 for rank in range(2, count + 1)]
    spare, holding = total - most - (count - 1), [1] * (count - 1)
    while spare > 0:
        free = [i for i in range(count - 1) if holding[i] < most]
        pool, budget = sum([portions[i] for i in free]), spare
        for i in free:
            addition = min(most - holding[i], max(1, budget * portions[i] // pool), spare)
            holding[i] = holding[i] + addition
            spare = spare - addition
    return np.array([most] + holding)


def uneven(own_key, number_of, total, limit, slope):
    if number_of == 2:
        one = jax.random.randint(own_key, (), max(1, total - limit), min(limit, total - 1) + 1)
        return jnp.stack([one, total - one])
    tallies = jnp.asarray(length_profile(number_of, total, limit, slope), jnp.int32)
    pairs = (number_of - 1) // 2
    source_of, taker = tallies[1:1 + 2 * pairs:2], tallies[2:2 + 2 * pairs:2]
    margin = jnp.minimum(source_of - 1, limit - taker)
    shifted = jax.random.randint(jax.random.fold_in(own_key, 1), (pairs,), 0, 1 << 20) % (margin + 1)
    tallies = tallies.at[1:1 + 2 * pairs:2].set(source_of - shifted).at[2:2 + 2 * pairs:2].set(taker + shifted)
    return tallies[jax.random.permutation(jax.random.fold_in(own_key, 2), number_of)]


def normal_values(key, dims, scale, most, cuts=(), kind=jnp.bfloat16):
    array = scale * jax.random.normal(key, dims, jnp.float32)
    if cuts:
        array = array * block_levels(key, dims, cuts, -0.22, 0.18)
    return jnp.clip(array, -most, most).astype(kind)


def setup_inputs(seed: int = 0) -> dict:
    key_of = jax.random.split(jax.random.key(seed), 13)
    return {
        "activations": draw_activations(jax.random.fold_in(key_of[12], 71), 0),
        "segment_ids": jax.vmap(lambda own: jnp.searchsorted(jnp.cumsum(uneven(own, 3, LENGTH, 3 * LENGTH // 4, 1)), jnp.arange(LENGTH), side="right"))(jax.random.split(key_of[1], SEQS)).reshape((SEQS, LENGTH)).astype(jnp.int32),
        "attention_gain": jnp.clip(1.0 + 0.1 * jax.random.normal(key_of[2], (D,), jnp.float32), 0.5, 1.5),
        "query_weight": draw_query_weight(jax.random.fold_in(key_of[12], 71), 0),
        "key_weight": draw_key_weight(jax.random.fold_in(key_of[12], 71), 0),
        "value_weight": normal_values(key_of[5], (D, KVW), D ** -0.5, 0.1875, ((0, 8), (1, 4))),
        "output_weight": normal_values(key_of[6], (D, D), (D // 16) ** -0.5, 0.75, ((0, 8), (1, 4))),
        "feed_gain": jnp.clip(1.0 + 0.1 * jax.random.normal(key_of[7], (D,), jnp.float32), 0.5, 1.5),
        "gate_weight": normal_values(key_of[8], (D, FF), D ** -0.5, 0.1875, ((0, 8), (1, 4))),
        "up_weight": normal_values(key_of[9], (D, FF), D ** -0.5, 0.1875, ((0, 8), (1, 4))),
        "down_weight": normal_values(key_of[10], (FF, D), FF ** -0.5, 0.125, ((0, 4), (1, 8))),
        "out_grad": normal_values(key_of[11], (SEQS, LENGTH, D), 1.0, 6.0, ((0, 8), (1, 4)), jnp.float32),
    }


def rotary_tables(positions):
    half = HEAD_DIM // 2
    expon = jnp.arange(half, dtype=jnp.float32) * (2.0 / HEAD_DIM)
    inverse = jnp.power(jnp.float32(10000.0), -expon)
    angles = positions[:, None] * inverse[None, :]
    return (jnp.cos(angles), jnp.sin(angles))

def rotate(tensor, cosine, sine):
    half = tensor.shape[-1] // 2
    first = tensor[..., :half]
    second = tensor[..., half:]
    cos_b = cosine[:, None, :]
    sin_b = sine[:, None, :]
    return jnp.concatenate([first * cos_b - second * sin_b, second * cos_b + first * sin_b], -1)

def rotate_back(tensor, cosine, sine):
    half = tensor.shape[-1] // 2
    first = tensor[..., :half]
    second = tensor[..., half:]
    cos_b = cosine[:, None, :]
    sin_b = sine[:, None, :]
    return jnp.concatenate([first * cos_b + second * sin_b, second * cos_b - first * sin_b], -1)

def rms_scale(rows):
    return lax.rsqrt(lax.optimization_barrier(jnp.mean(rows * rows, -1, keepdims=True)) + 1e-05)

def norm_back(grad_out, normed, scale, gain):
    scaled = grad_out * gain
    inner = lax.optimization_barrier(jnp.mean(scaled * normed, -1, keepdims=True))
    return (scale * (scaled - normed * inner), lax.optimization_barrier(jnp.sum(grad_out * normed, 0)))

def mmul(left, right):
    return jnp.dot(left, right, preferred_element_type=jnp.float32)

def one_sequence(rows, seg_row, grad_rows, weights, gains, cosine, sine):
    query_weight, key_weight, value_weight, output_weight, gate_weight, up_weight, down_weight = weights
    attention_gain, feed_gain = gains
    length = rows.shape[0]
    groups = HEADS // KV_HEADS
    inv_root = 1.0 / HEAD_DIM ** 0.5
    scale_attn = rms_scale(rows)
    normed_attn = rows * scale_attn
    hidden_attn = (normed_attn * attention_gain).astype(jnp.bfloat16)
    query_rot = rotate(mmul(hidden_attn, query_weight).reshape(length, HEADS, HEAD_DIM), cosine, sine).astype(jnp.bfloat16)
    key_rot = rotate(mmul(hidden_attn, key_weight).reshape(length, KV_HEADS, HEAD_DIM), cosine, sine).astype(jnp.bfloat16)
    value_rows = mmul(hidden_attn, value_weight).astype(jnp.bfloat16)
    query_group = query_rot.reshape(length, KV_HEADS, groups, HEAD_DIM).astype(jnp.float32)
    key_group = key_rot.astype(jnp.float32)
    value_group = value_rows.reshape(length, KV_HEADS, HEAD_DIM).astype(jnp.float32)
    order = jnp.arange(length, dtype=jnp.int32)
    allowed = (seg_row[:, None] == seg_row[None, :]) & (order[None, :] <= order[:, None])
    scores = jnp.einsum('nkgd,mkd->kgnm', query_group, key_group) * inv_root
    scores = jnp.where(allowed[None, None], scores, -jnp.inf)
    top = lax.optimization_barrier(jnp.max(scores, -1, keepdims=True))
    log_total = top + jnp.log(lax.optimization_barrier(jnp.sum(jnp.exp(scores - top), -1, keepdims=True)))
    probs = jnp.exp(scores - log_total)
    probs_low = probs.astype(jnp.bfloat16)
    attn_rows = jnp.einsum('kgnm,mkd->nkgd', probs_low.astype(jnp.float32), value_group)
    attn_rows = attn_rows.reshape(length, D).astype(jnp.bfloat16)
    mid_rows = rows + mmul(attn_rows, output_weight)
    scale_feed = rms_scale(mid_rows)
    normed_feed = mid_rows * scale_feed
    hidden_feed = (normed_feed * feed_gain).astype(jnp.bfloat16)
    gate_rows = mmul(hidden_feed, gate_weight)
    up_rows = mmul(hidden_feed, up_weight)
    sigma = jax.nn.sigmoid(gate_rows)
    inner_rows = (gate_rows * sigma * up_rows).astype(jnp.bfloat16)
    block_output = mid_rows + mmul(inner_rows, down_weight)
    grad_low = grad_rows.astype(jnp.bfloat16)
    down_grad = mmul(inner_rows.T, grad_low)
    grad_inner = mmul(grad_low, down_weight.T)
    grad_up = (grad_inner * gate_rows * sigma).astype(jnp.bfloat16)
    grad_gate = (grad_inner * up_rows * sigma * (1.0 + gate_rows * (1.0 - sigma))).astype(jnp.bfloat16)
    gate_grad = mmul(hidden_feed.T, grad_gate)
    up_grad = mmul(hidden_feed.T, grad_up)
    grad_hidden_feed = mmul(grad_gate, gate_weight.T) + mmul(grad_up, up_weight.T)
    back_feed, feed_gain_term = norm_back(grad_hidden_feed, normed_feed, scale_feed, feed_gain)
    grad_mid = grad_rows + back_feed
    grad_mid_low = grad_mid.astype(jnp.bfloat16)
    output_grad = mmul(attn_rows.T, grad_mid_low)
    grad_attn = mmul(grad_mid_low, output_weight.T).astype(jnp.bfloat16)
    grad_attn_group = grad_attn.reshape(length, KV_HEADS, groups, HEAD_DIM).astype(jnp.float32)
    attn_group = attn_rows.reshape(length, KV_HEADS, groups, HEAD_DIM).astype(jnp.float32)
    grad_probs = jnp.einsum('nkgd,mkd->kgnm', grad_attn_group, value_group)
    row_dots = jnp.transpose(lax.optimization_barrier(jnp.sum(grad_attn_group * attn_group, -1)), (1, 2, 0))
    grad_scores = (probs * (grad_probs - row_dots[..., None]) * inv_root).astype(jnp.bfloat16)
    grad_scores_f = grad_scores.astype(jnp.float32)
    grad_query = jnp.einsum('kgnm,mkd->nkgd', grad_scores_f, key_group).reshape(length, HEADS, HEAD_DIM)
    grad_query = rotate_back(grad_query, cosine, sine).reshape(length, D).astype(jnp.bfloat16)
    grad_key = jnp.einsum('kgnm,nkgd->mkd', grad_scores_f, query_group)
    grad_key = rotate_back(grad_key, cosine, sine).reshape(length, KVW).astype(jnp.bfloat16)
    grad_value = jnp.einsum('kgnm,nkgd->mkd', probs_low.astype(jnp.float32), grad_attn_group)
    grad_value = grad_value.reshape(length, KVW).astype(jnp.bfloat16)
    query_grad = mmul(hidden_attn.T, grad_query)
    key_grad = mmul(hidden_attn.T, grad_key)
    value_grad = mmul(hidden_attn.T, grad_value)
    grad_hidden_attn = mmul(grad_query, query_weight.T) + mmul(grad_key, key_weight.T) + mmul(grad_value, value_weight.T)
    back_attn, attn_gain_term = norm_back(grad_hidden_attn, normed_attn, scale_attn, attention_gain)
    input_grad = grad_mid + back_attn
    grads = (query_grad, key_grad, value_grad, output_grad, gate_grad, up_grad, down_grad)
    return (block_output, input_grad, grads, (attn_gain_term, feed_gain_term))

def reference(activations, segment_ids, attention_gain, query_weight, key_weight, value_weight, output_weight, feed_gain, gate_weight, up_weight, down_weight, out_grad):
    weights = (query_weight, key_weight, value_weight, output_weight, gate_weight, up_weight, down_weight)
    gains = (attention_gain, feed_gain)
    positions = jnp.arange(LENGTH, dtype=jnp.int32).astype(jnp.float32)
    cosine, sine = rotary_tables(positions)
    init_grads = tuple((jnp.zeros(w.shape, jnp.float32) for w in weights))
    init_gains = (jnp.zeros((D,), jnp.float32), jnp.zeros((D,), jnp.float32))

    def advance(carry, inputs):
        sum_grads, sum_gains = carry
        rows, seg_row, grad_rows = inputs
        block_output, input_grad, grads, gain_terms = one_sequence(rows, seg_row, grad_rows, weights, gains, cosine, sine)
        sum_grads = tuple((a + b for a, b in zip(sum_grads, grads)))
        sum_gains = tuple((a + b for a, b in zip(sum_gains, gain_terms)))
        return ((sum_grads, sum_gains), (block_output, input_grad))
    carry, stacked = lax.scan(advance, (init_grads, init_gains), (activations, segment_ids, out_grad))
    sum_grads, sum_gains = carry
    block_output, input_grad = stacked
    return (block_output, input_grad, sum_gains[0], sum_grads[0], sum_grads[1], sum_grads[2], sum_grads[3], sum_gains[1], sum_grads[4], sum_grads[5], sum_grads[6])
```

```python
import jax
import jax.numpy as jnp
from jax import lax
from jax.sharding import PartitionSpec as P

HEADS = 15
KV_HEADS = 5
HEAD_DIM = 64
BF = jnp.bfloat16
F32 = jnp.float32


def rotary_tables(positions):
    half = HEAD_DIM // 2
    expon = jnp.arange(half, dtype=F32) * (2.0 / HEAD_DIM)
    inverse = jnp.power(F32(10000.0), -expon)
    angles = positions[:, None] * inverse[None, :]
    return (jnp.cos(angles), jnp.sin(angles))


def rotate(tensor, cosine, sine):
    half = tensor.shape[-1] // 2
    first = tensor[..., :half]
    second = tensor[..., half:]
    cos_b = cosine[:, None, :]
    sin_b = sine[:, None, :]
    return jnp.concatenate([first * cos_b - second * sin_b, second * cos_b + first * sin_b], -1)


def rotate_back(tensor, cosine, sine):
    return rotate(tensor, cosine, -sine)


def rms_scale(rows):
    return lax.rsqrt(jnp.mean(rows * rows, -1, keepdims=True) + 1e-05)


def norm_back(grad_out, normed, scale, gain):
    scaled = grad_out * gain
    inner = jnp.mean(scaled * normed, -1, keepdims=True)
    return (scale * (scaled - normed * inner), jnp.sum(grad_out * normed, 0))


def mmul(left, right):
    return jnp.dot(left, right, preferred_element_type=F32)


def left_mmul(left, right):
    return lax.dot_general(left, right, (((0,), (0,)), ((), ())), preferred_element_type=F32)


def right_mmul(left, right):
    return lax.dot_general(left, right, (((1,), (1,)), ((), ())), preferred_element_type=F32)


def flip(x, bits):
    n = lax.axis_size("batch")
    return lax.ppermute(x, "batch", [(i, i ^ bits) for i in range(n)])


def chips():
    return lax.axis_size("batch") // 2


def shift(x, by):
    n = lax.axis_size("seq")
    return lax.ppermute(x, "seq", [(i, (i + by) % n) for i in range(n)])


def push(x, by):
    n = lax.axis_size("seq")
    pairs = [(i, i + by) for i in range(n) if 0 <= i + by < n]
    return lax.ppermute(x, "seq", pairs)


def pick(stack, at):
    return lax.dynamic_index_in_dim(stack, at, 0, keepdims=False)


def line_gather(x):
    n = lax.axis_size("seq")
    return jnp.stack([x] + [shift(x, -k) for k in range(1, n)])


def line_scatter(parts):
    n = lax.axis_size("seq")
    own = parts[0]
    for k in range(1, n):
        own = own + shift(parts[k].astype(BF), k).astype(F32)
    return own


def line_order(stack):
    n = stack.shape[0]
    s = lax.axis_index("seq")
    return lax.dynamic_slice_in_dim(jnp.concatenate([stack, stack], 0), n - s, n, 0)


def plane_gather(x):
    mine = jnp.stack([x] + [flip(x, 2 * m) for m in range(1, chips())])
    return jnp.stack([mine, flip(mine, 1)])


def plane_scatter(near, far):
    both = near + flip(far.astype(BF), 1).astype(F32)
    own = both[0]
    for m in range(1, chips()):
        own = own + flip(both[m].astype(BF), 2 * m).astype(F32)
    return own


def whole_weight(blocks):
    n = lax.axis_size("seq")
    b = lax.axis_index("batch")
    rows = blocks[0].shape[0]
    widths = [w.shape[1] for w in blocks]
    slots = line_order(line_gather(jnp.concatenate(blocks, 1) if len(blocks) > 1 else blocks[0]))
    parts = []
    start = 0
    for width in widths:
        parts.append(jnp.concatenate([slots[p, :, start : start + width] for p in range(n)], 1))
        start += width
    wide = jnp.concatenate(parts, 1) if len(parts) > 1 else parts[0]
    got = plane_gather(wide)
    size = lax.axis_size("batch")
    out = jnp.zeros((size, rows, wide.shape[1]), wide.dtype)
    for core in range(2):
        for m in range(chips()):
            out = lax.dynamic_update_index_in_dim(out, got[core, m], b ^ (2 * m + core), 0)
    return out.reshape(size * rows, wide.shape[1])


def weight_scatter(terms):
    n = lax.axis_size("seq")
    size = lax.axis_size("batch")
    b = lax.axis_index("batch")
    s = lax.axis_index("seq")
    wide = jnp.concatenate(terms, 1) if len(terms) > 1 else terms[0]
    rows = wide.shape[0] // size
    cut = wide.reshape(size, rows, wide.shape[1])
    near = jnp.stack([pick(cut, b ^ (2 * m)) for m in range(chips())])
    far = jnp.stack([pick(cut, b ^ (2 * m + 1)) for m in range(chips())])
    mine = plane_scatter(near, far)
    start = 0
    pieces = []
    for term in terms:
        width = term.shape[1] // n
        pieces.append([mine[:, start + p * width : start + (p + 1) * width] for p in range(n)])
        start += term.shape[1]
    stack = jnp.stack([jnp.concatenate([q[p] for q in pieces], 1) for p in range(n)])
    own = line_scatter([pick(stack, (s + k) % n) for k in range(n)])
    out = []
    start = 0
    for term in terms:
        width = term.shape[1] // n
        out.append(own[:, start : start + width])
        start += width
    return out


def total(x):
    n = lax.axis_size("batch")
    bits = 1
    while bits < n:
        x = x + flip(x, bits)
        bits *= 2
    n = lax.axis_size("seq")
    bits = 1
    while bits < n:
        x = x + lax.ppermute(x, "seq", [(i, i ^ bits) for i in range(n)])
        bits *= 2
    return x


def shards(
    activations,
    segment_ids,
    attention_gain,
    query_weight,
    key_weight,
    value_weight,
    output_weight,
    feed_gain,
    gate_weight,
    up_weight,
    down_weight,
    out_grad,
):
    piece, width = activations.shape[1:]
    line = lax.axis_size("seq")
    size = lax.axis_size("batch")
    length = piece * line
    groups = HEADS // KV_HEADS
    kv_width = KV_HEADS * HEAD_DIM
    inv_root = 1.0 / HEAD_DIM**0.5
    rows = activations[0]
    grad_rows = out_grad[0]
    s = lax.axis_index("seq")
    positions = s * piece + jnp.arange(piece, dtype=jnp.int32)
    cosine, sine = rotary_tables(positions.astype(F32))

    kv_full = whole_weight([key_weight, value_weight])
    query_full = whole_weight([query_weight])
    output_full = whole_weight([output_weight])

    units = gate_weight.shape[1] // size
    local = jnp.stack([gate_weight.T, up_weight.T, down_weight])
    local = local.reshape(3, size, units, local.shape[2]).transpose(1, 0, 2, 3)
    spread = lax.all_to_all(local, "batch", split_axis=0, concat_axis=0, tiled=True)
    spread = spread.transpose(1, 2, 0, 3).reshape(3 * units, width)
    feed = line_gather(spread).reshape(line, 3, units, width)
    gate_part = feed[:, 0].reshape(line * units, width)
    up_part = feed[:, 1].reshape(line * units, width)
    down_part = feed[:, 2].reshape(line * units, width)

    grad_low = grad_rows.astype(BF)
    grad_low_all = plane_gather(grad_low).reshape(size * piece, width)

    scale_attn = rms_scale(rows)
    normed_attn = rows * scale_attn
    hidden_attn = (normed_attn * attention_gain).astype(BF)
    kv_rows = mmul(hidden_attn, kv_full)
    key_rot = rotate(kv_rows[:, :kv_width].reshape(piece, KV_HEADS, HEAD_DIM), cosine, sine)
    key_rot = key_rot.reshape(piece, kv_width).astype(BF)
    value_rows = kv_rows[:, kv_width:].astype(BF)
    query_rot = rotate(
        mmul(hidden_attn, query_full).reshape(piece, HEADS, HEAD_DIM), cosine, sine
    ).astype(BF)

    seg_local = segment_ids.astype(BF)
    seg_row = jnp.pad(seg_local, ((0, 7), (0, 2 * kv_width - piece)))
    packet = jnp.concatenate([jnp.concatenate([key_rot, value_rows], 1), seg_row], 0)
    packets = jnp.stack([packet] + [push(packet, k) for k in range(1, line)])
    key_all = packets[:, :piece, :kv_width].reshape(length, kv_width)
    value_all = packets[:, :piece, kv_width:].reshape(length, kv_width)
    seg_all = packets[:, piece, :piece].reshape(length)
    key_at = (s - jnp.arange(line, dtype=jnp.int32))[:, None] * piece + jnp.arange(
        piece, dtype=jnp.int32
    )
    key_at = key_at.reshape(length)

    query_group = query_rot.reshape(piece, KV_HEADS, groups, HEAD_DIM)
    key_group = key_all.reshape(length, KV_HEADS, HEAD_DIM)
    value_group = value_all.reshape(length, KV_HEADS, HEAD_DIM)
    allowed = (
        (seg_local[0][:, None] == seg_all[None, :])
        & (key_at[None, :] <= positions[:, None])
        & (key_at[None, :] >= 0)
    )
    scores = (
        jnp.einsum("nkgd,mkd->kgnm", query_group, key_group, preferred_element_type=F32) * inv_root
    )
    scores = jnp.where(allowed[None, None], scores, -jnp.inf)
    top = jnp.max(scores, -1, keepdims=True)
    log_total = top + jnp.log(jnp.sum(jnp.exp(scores - top), -1, keepdims=True))
    probs = jnp.exp(scores - log_total)
    probs_low = probs.astype(BF)
    attn_rows = jnp.einsum("kgnm,mkd->nkgd", probs_low, value_group, preferred_element_type=F32)
    attn_rows = attn_rows.reshape(piece, width).astype(BF)
    mid_rows = rows + mmul(attn_rows, output_full)
    scale_feed = rms_scale(mid_rows)
    normed_feed = mid_rows * scale_feed
    hidden_feed = (normed_feed * feed_gain).astype(BF)

    hidden_feed_all = plane_gather(hidden_feed).reshape(size * piece, width)
    gate_rows = right_mmul(hidden_feed_all, gate_part)
    up_rows = right_mmul(hidden_feed_all, up_part)
    sigma = jax.nn.sigmoid(gate_rows)
    inner_rows = (gate_rows * sigma * up_rows).astype(BF)
    grad_inner = right_mmul(grad_low_all, down_part)
    grad_up = (grad_inner * gate_rows * sigma).astype(BF)
    grad_gate = (grad_inner * up_rows * sigma * (1.0 + gate_rows * (1.0 - sigma))).astype(BF)
    half = size // 2
    back = (mmul(grad_gate, gate_part) + mmul(grad_up, up_part)).reshape(2, half, piece, width)
    grad_hidden_feed = plane_scatter(back[0], back[1])
    down_rows = mmul(inner_rows, down_part).reshape(2, half, piece, width)
    block_output = mid_rows + plane_scatter(down_rows[0], down_rows[1])

    gate_grad = left_mmul(grad_gate, hidden_feed_all).reshape(line, units, width)
    up_grad = left_mmul(grad_up, hidden_feed_all).reshape(line, units, width)
    down_grad = left_mmul(inner_rows, grad_low_all).reshape(line, units, width)
    terms = jnp.concatenate([gate_grad, up_grad, down_grad], 1)
    feed_own = line_scatter([terms[k] for k in range(line)]).astype(BF)
    feed_own = feed_own.reshape(3 * units, size, width // size).transpose(1, 0, 2)
    feed_back = lax.all_to_all(feed_own, "batch", split_axis=0, concat_axis=0, tiled=True)
    feed_back = feed_back.reshape(size, 3, units, width // size).transpose(1, 0, 2, 3)
    feed_back = feed_back.reshape(3, size * units, width // size).astype(F32)
    gate_done = feed_back[0].T
    up_done = feed_back[1].T
    down_done = feed_back[2]

    back_feed, feed_gain_term = norm_back(grad_hidden_feed, normed_feed, scale_feed, feed_gain)
    grad_mid = grad_rows + back_feed
    grad_mid_low = grad_mid.astype(BF)
    (output_done,) = weight_scatter([left_mmul(attn_rows, grad_mid_low)])
    grad_attn = right_mmul(grad_mid_low, output_full).astype(BF)
    grad_attn_group = grad_attn.reshape(piece, KV_HEADS, groups, HEAD_DIM)
    attn_group = attn_rows.reshape(piece, KV_HEADS, groups, HEAD_DIM)
    grad_probs = jnp.einsum(
        "nkgd,mkd->kgnm", grad_attn_group, value_group, preferred_element_type=F32
    )
    row_dots = jnp.einsum("nkgd,nkgd->kgn", grad_attn_group, attn_group, preferred_element_type=F32)
    grad_scores = (probs * (grad_probs - row_dots[..., None]) * inv_root).astype(BF)
    key_term = jnp.einsum("kgnm,nkgd->mkd", grad_scores, query_group, preferred_element_type=F32)
    value_term = jnp.einsum("kgnm,nkgd->mkd", probs_low, grad_attn_group, preferred_element_type=F32)
    both_terms = jnp.concatenate(
        [key_term.reshape(line, piece, kv_width), value_term.reshape(line, piece, kv_width)], -1
    )
    both_grads = both_terms[0]
    for k in range(1, line):
        both_grads = both_grads + push(both_terms[k].astype(BF), -k).astype(F32)
    grad_query = jnp.einsum("kgnm,mkd->nkgd", grad_scores, key_group, preferred_element_type=F32)
    grad_query = (
        rotate_back(grad_query.reshape(piece, HEADS, HEAD_DIM), cosine, sine)
        .reshape(piece, width)
        .astype(BF)
    )
    (query_done,) = weight_scatter([left_mmul(hidden_attn, grad_query)])
    grad_key = rotate_back(
        both_grads[:, :kv_width].reshape(piece, KV_HEADS, HEAD_DIM), cosine, sine
    )
    grad_kv = jnp.concatenate(
        [grad_key.reshape(piece, kv_width).astype(BF), both_grads[:, kv_width:].astype(BF)], 1
    )
    kv_grad = left_mmul(hidden_attn, grad_kv)
    key_done, value_done = weight_scatter([kv_grad[:, :kv_width], kv_grad[:, kv_width:]])
    grad_hidden_attn = right_mmul(grad_query, query_full) + right_mmul(grad_kv, kv_full)
    back_attn, attn_gain_term = norm_back(grad_hidden_attn, normed_attn, scale_attn, attention_gain)
    input_grad = grad_mid + back_attn
    gains = total(jnp.stack([attn_gain_term, feed_gain_term]))
    return (
        block_output[None],
        input_grad[None],
        gains[0],
        query_done,
        key_done,
        value_done,
        output_done,
        gains[1],
        gate_done,
        up_done,
        down_done,
    )


def solution(mesh):
    both = P("batch", "seq")
    tokens = P("batch", "seq", None)
    in_specs = (tokens, both, P(), both, both, both, both, P(), both, both, P("seq", "batch"), tokens)
    out_specs = (tokens, tokens, P(), both, both, both, both, P(), both, both, P("seq", "batch"))
    return jax.shard_map(shards, mesh=mesh, in_specs=in_specs, out_specs=out_specs, check_vma=False)
```

```python
import functools
import math

import jax
import jax.numpy as jnp
from jax import lax
from jax.experimental import pallas as pl
from jax.experimental.pallas import tpu as pltpu
from jax.sharding import PartitionSpec as P


HEADS = 15
KV_HEADS = 5
HEAD_DIM = 64
GROUPS = HEADS // KV_HEADS
KV_WIDTH = KV_HEADS * HEAD_DIM
HALF = HEAD_DIM // 2
INV_ROOT = 1.0 / HEAD_DIM**0.5
BF = jnp.bfloat16
F32 = jnp.float32
ROOM = 6


def rotary_tables(positions):
    expon = jnp.arange(HALF, dtype=F32) * (2.0 / HEAD_DIM)
    inverse = jnp.power(F32(10000.0), -expon)
    angles = positions[:, None] * inverse[None, :]
    return jnp.cos(angles), jnp.sin(angles)


def mmul(left, right):
    return jnp.dot(left, right, preferred_element_type=F32)


def left_mmul(left, right):
    return lax.dot_general(left, right, (((0,), (0,)), ((), ())), preferred_element_type=F32)


def right_mmul(left, right):
    return lax.dot_general(left, right, (((1,), (1,)), ((), ())), preferred_element_type=F32)


def head_of(h):
    return slice(h * HEAD_DIM, (h + 1) * HEAD_DIM)


def tables(cosine, sine):
    c, d = cosine[...], sine[...]
    return jnp.concatenate([c, c], 1), jnp.concatenate([-d, d], 1)


def swapped(x):
    return jnp.concatenate([x[:, HALF:], x[:, :HALF]], 1)


def rms_scale(rows):
    return lax.rsqrt(jnp.mean(rows * rows, -1, keepdims=True) + 1e-05)


def norm_back(grad_out, normed, scale, gain):
    scaled = grad_out * gain
    inner = jnp.mean(scaled * normed, -1, keepdims=True)
    return (scale * (scaled - normed * inner), jnp.sum(grad_out * normed, 0, keepdims=True))


def split_lanes(ref, value, count):
    wide = value.shape[1] // count
    for j in range(count):
        ref[j] = value[:, j * wide : (j + 1) * wide]


def join_lanes(ref, count):
    return jnp.concatenate([ref[j] for j in range(count)], 1)


def blocks(near, far):
    b = lax.axis_index("batch")
    out = []
    for core, refs in ((0, near), (1, far)):
        for m, ref in enumerate(refs):
            out.append((ref, core, m, b ^ (2 * m + core)))
    return out


def take(refs, *counts):
    out = []
    at = 0
    for n in counts:
        out.append(refs[at] if n is None else refs[at : at + n])
        at += 1 if n is None else n
    assert at == len(refs)
    return out


def kv_kernel(chips, *refs):
    rows, gain, cosine, sine, seg, near, far, hidden, packet, hid3, acc4 = take(
        refs, *[None] * 5, chips, chips, *[None] * 4
    )
    line = near[0].shape[0]
    s = lax.axis_index("seq")
    piece = rows.shape[1]
    cos, sin = tables(cosine, sine)
    x = rows[...].T
    hid = (x * rms_scale(x) * gain[...]).astype(BF)
    hidden[...] = hid
    split_lanes(hid3, hid, hid3.shape[0])
    for k in range(line):
        acc = 0.0
        for ref, _, m, at in blocks(near, far):
            acc = acc + mmul(hid3[at], ref[k])
        acc4[s ^ k] = acc
    wide = near[0].shape[-1] // 2
    keys = jnp.concatenate([acc4[p, :, :wide] for p in range(line)], 1)
    values = jnp.concatenate([acc4[p, :, wide:] for p in range(line)], 1)
    for h in range(KV_HEADS):
        u = keys[:, head_of(h)]
        packet[:piece, head_of(h)] = (u * cos + swapped(u) * sin).astype(BF)
    packet[:piece, KV_WIDTH:] = values.astype(BF)
    packet[piece:, :] = jnp.zeros((packet.shape[0] - piece, packet.shape[1]), BF)
    packet[piece:, :piece] = jnp.broadcast_to(
        seg[...].astype(F32), (packet.shape[0] - piece, piece)
    ).astype(BF)


def query_kernel(chips, *refs):
    hidden, cosine, sine, near, far, query, hid3, acc4 = take(
        refs, None, None, None, chips, chips, None, None, None
    )
    line = near[0].shape[0]
    s = lax.axis_index("seq")
    cos, sin = tables(cosine, sine)
    split_lanes(hid3, hidden[...], hid3.shape[0])
    for k in range(line):
        acc = 0.0
        for ref, _, m, at in blocks(near, far):
            acc = acc + mmul(hid3[at], ref[k, 0])
        acc4[s ^ k] = acc
    full = join_lanes(acc4, line)
    for h in range(HEADS):
        u = full[:, head_of(h)]
        query[:, head_of(h)] = (u * cos + swapped(u) * sin).astype(BF)


def group_rows(ref, g):
    return jnp.concatenate([ref[:, head_of(GROUPS * g + i)] for i in range(GROUPS)], 0)


def slot_rows(packets, piece, lanes):
    return jnp.concatenate([p[:piece, lanes] for p in packets], 0)


def attention_kernel(chips, line, *refs):
    query, packets, rows, seg, gain, near, far, *rest = take(
        refs, None, line, None, None, None, chips, chips, *[None] * 7
    )
    probs, attn, mid, hidden, bias, att3, acc4 = rest
    s = lax.axis_index("seq")
    piece = rows.shape[1]
    mine = jnp.broadcast_to(seg[...].astype(F32), (piece, piece)).T
    at = lax.broadcasted_iota(jnp.int32, (piece, piece), 0)
    key = lax.broadcasted_iota(jnp.int32, (piece, piece), 1)
    for k in range(line):
        same = mine == packets[k][piece : piece + 1, :piece].astype(F32)
        ok = same & (key - k * piece <= at) & (key + (s - k) * piece >= 0)
        bias[:, k * piece : (k + 1) * piece] = jnp.where(ok, 0.0, -jnp.inf)
    for g in range(KV_HEADS):
        keys = slot_rows(packets, piece, head_of(g))
        values = slot_rows(packets, piece, head_of(KV_HEADS + g))
        scores = right_mmul(group_rows(query, g), keys) * INV_ROOT
        scores = scores + jnp.concatenate([bias[...]] * GROUPS, 0)
        raised = jnp.exp(scores - jnp.max(scores, -1, keepdims=True))
        weights = raised / jnp.sum(raised, -1, keepdims=True)
        probs[g] = weights
        out = mmul(weights.astype(BF), values).astype(BF)
        for i in range(GROUPS):
            attn[:, head_of(GROUPS * g + i)] = out[i * piece : (i + 1) * piece]
    split_lanes(att3, attn[...], att3.shape[0])
    for k in range(line):
        acc = 0.0
        for ref, _, m, j in blocks(near, far):
            acc = acc + mmul(att3[j], ref[k, 1])
        acc4[s ^ k] = acc
    x = rows[...].T + join_lanes(acc4, line)
    mid[...] = x
    hidden[...] = (x * rms_scale(x) * gain[...]).astype(BF)


def load_all(refs, scratch, sems):
    rows = refs[0].shape[0]
    copies = [
        pltpu.make_async_copy(ref, scratch.at[pl.ds(i * rows, rows)], sems.at[i])
        for i, ref in enumerate(refs)
    ]
    for copy in copies:
        copy.start()
    return copies


def load_slots(own, right, left, slots):
    s = lax.axis_index("seq")
    line = slots.shape[0]
    pltpu.sync_copy(own, slots.at[0])
    for k in range(1, line):
        for far in range(1, line):

            @pl.when((s ^ k) == s - far)
            def _():
                pltpu.sync_copy(right[far - 1], slots.at[k])

            @pl.when((s ^ k) == s + far)
            def _():
                pltpu.sync_copy(left[far - 1], slots.at[k])


def feed_kernel(chips, line, tile, *refs):
    hid, low, own, right, left, back_near, back_far, gate_s, up_s, inner_s, *scratch = take(
        refs, 2 * chips, 2 * chips, None, line - 1, line - 1, None, chips, *[None] * 12
    )
    slots, gate_w, up_w, down_w, hid_s, low_s, far_s, sems, far_sems = scratch
    copies = load_all(hid, hid_s, sems) + load_all(low, low_s, sems.at[pl.ds(2 * chips, 2 * chips)])
    load_slots(own, right, left, slots)
    piece = hid[0].shape[0]
    units = own.shape[0] // 3
    for k in range(line):
        span = slice(k * units, (k + 1) * units)
        gate_w[span] = slots[k, :units]
        up_w[span] = slots[k, units : 2 * units]
        down_w[span] = slots[k, 2 * units :]
    for copy in copies:
        copy.wait()
    half = chips * piece

    def run(back, base):
        def body(i, carry):
            span = pl.ds(pl.multiple_of(i * tile, tile), tile)
            read = pl.ds(pl.multiple_of(base + i * tile, tile), tile)
            h = hid_s[read]
            gate = right_mmul(h, gate_w[...])
            up = right_mmul(h, up_w[...])
            inner_grad = right_mmul(low_s[read], down_w[...])
            sigma = jax.nn.sigmoid(gate)
            inner_s[read] = (gate * sigma * up).astype(BF)
            grad_up = (inner_grad * gate * sigma).astype(BF)
            grad_gate = (inner_grad * up * sigma * (1.0 + gate * (1.0 - sigma))).astype(BF)
            gate_s[read] = grad_gate
            up_s[read] = grad_up
            total_back = mmul(grad_gate, gate_w[...]) + mmul(grad_up, up_w[...])
            back[span] = total_back.astype(BF)
            return carry

        lax.fori_loop(0, half // tile, body, 0)

    run(far_s, half)
    sends = [
        pltpu.make_async_copy(far_s.at[pl.ds(m * piece, piece)], back_far[m], far_sems.at[m])
        for m in range(chips)
    ]
    for send in sends:
        send.start()
    run(back_near, 0)
    for send in sends:
        send.wait()


def feed_grad_kernel(chips, line, *refs):
    hid, low, own, right, left, gate_s, up_s, inner_s, down_near, down_far, grads, *scratch = take(
        refs, 2 * chips, 2 * chips, None, line - 1, line - 1, *[None] * 4, chips, line, *[None] * 5
    )
    slots, down_w, hid_s, low_s, sems = scratch
    copies = load_all(hid, hid_s, sems) + load_all(low, low_s, sems.at[pl.ds(2 * chips, 2 * chips)])
    load_slots(own, right, left, slots)
    piece = hid[0].shape[0]
    units = own.shape[0] // 3
    for k in range(line):
        down_w[k * units : (k + 1) * units] = slots[k, 2 * units :]
    for copy in copies:
        copy.wait()
    half = chips * piece
    for m in range(chips):
        span = slice(m * piece, (m + 1) * piece)
        far = slice(half + m * piece, half + (m + 1) * piece)
        down_near[span] = mmul(inner_s[span], down_w[...]).astype(BF)
        down_far[m][...] = mmul(inner_s[far], down_w[...]).astype(BF)
    for n, (a, b) in enumerate(((gate_s, hid_s), (up_s, hid_s), (inner_s, low_s))):
        term = left_mmul(a[...], b[...])
        for k in range(line):
            out = term[k * units : (k + 1) * units]
            grads[k][n * units : (n + 1) * units] = out.astype(grads[k].dtype)


def middle_kernel(chips, line, *refs):
    parts, mid, out_grad, gain, attn, query, probs, cosine, sine, near, far, packets, *rest = take(
        refs, chips, *[None] * 8, chips, chips, line, *[None] * 4, line, *[None] * 4
    )
    grad_mid, gain_term, grad_low, grad_query, slots, low4, att3, grad_attn, grad_kv = rest
    s = lax.axis_index("seq")
    piece = mid.shape[0]
    cos, sin = tables(cosine, sine)
    grad = parts[0][...].astype(F32)
    for part in parts[1:]:
        grad = grad + part[...].astype(F32)
    x = mid[...]
    scale = rms_scale(x)
    back, term = norm_back(grad, x * scale, scale, gain[...])
    gain_term[...] = term
    whole = out_grad[...].T + back
    grad_mid[...] = whole
    low = whole.astype(BF)
    grad_low[...] = low
    split_lanes(low4, low, line)
    for ref, _, m, j in blocks(near, far):
        acc = 0.0
        for k in range(line):
            acc = acc + right_mmul(low4[s ^ k], ref[k, 1])
        att3[j] = acc.astype(BF)
    grad_attn[...] = join_lanes(att3, att3.shape[0])
    for g in range(KV_HEADS):
        keys = slot_rows(packets, piece, head_of(g))
        values = slot_rows(packets, piece, head_of(KV_HEADS + g))
        q = group_rows(query, g)
        ga = group_rows(grad_attn, g)
        at = group_rows(attn, g)
        dots = jnp.sum(ga.astype(F32) * at.astype(F32), -1, keepdims=True)
        weights = probs[g]
        gs = (weights * (right_mmul(ga, values) - dots) * INV_ROOT).astype(BF)
        gq = mmul(gs, keys)
        for i in range(GROUPS):
            u = gq[i * piece : (i + 1) * piece]
            h = GROUPS * g + i
            grad_query[:, head_of(h)] = (u * cos - swapped(u) * sin).astype(BF)
        grad_kv[:, head_of(g)] = left_mmul(gs, q)
        grad_kv[:, head_of(KV_HEADS + g)] = left_mmul(weights.astype(BF), ga)
    for k in range(line):
        slots[k][...] = grad_kv[k * piece : (k + 1) * piece].astype(slots[k].dtype)


def query_grad_kernel(chips, *refs):
    hidden, grad_query, attn, grad_low, near, far, out_near, out_far, back, *scratch = take(
        refs, *[None] * 4, chips, chips, chips, chips, *[None] * 5
    )
    hid3, att3, gq4, low4 = scratch
    line = near[0].shape[0]
    s = lax.axis_index("seq")
    size = hid3.shape[0]
    split_lanes(hid3, hidden[...], size)
    split_lanes(att3, attn[...], size)
    split_lanes(gq4, grad_query[...], line)
    split_lanes(low4, grad_low[...], line)
    for ref, core, m, j in blocks(near, far):
        out = (out_near, out_far)[core][m]
        for k in range(line):
            out[k, 0] = left_mmul(hid3[j], gq4[s ^ k]).astype(BF)
            out[k, 1] = left_mmul(att3[j], low4[s ^ k]).astype(BF)
    for ref, _, m, j in blocks(near, far):
        acc = 0.0
        for k in range(line):
            acc = acc + right_mmul(gq4[s ^ k], ref[k, 0])
        back[j] = acc


def input_grad_kernel(chips, line, *refs):
    parts, rows, gain, hidden, grad_mid, base, cosine, sine, feed_term, near, far, *rest = take(
        refs, line, *[None] * 8, chips, chips, None, 2 * chips, *[None] * 4
    )
    result, outs, hid3, full, gkv4, x3 = take(rest, *[None] * 6)
    cos, sin = tables(cosine, sine)
    s = lax.axis_index("seq")
    size = hid3.shape[0]
    both = parts[0][...]
    for part in parts[1:]:
        both = both + part[...].astype(F32)
    for h in range(KV_HEADS):
        u = both[:, head_of(h)]
        full[:, head_of(h)] = (u * cos - swapped(u) * sin).astype(BF)
    full[:, KV_WIDTH:] = both[:, KV_WIDTH:].astype(BF)
    wide = KV_WIDTH // line
    for p in range(line):
        gkv4[p, :, :wide] = full[:, p * wide : (p + 1) * wide]
        gkv4[p, :, wide:] = full[:, KV_WIDTH + p * wide : KV_WIDTH + (p + 1) * wide]
    split_lanes(hid3, hidden[...], size)
    for ref, _, m, j in blocks(near, far):
        acc = base[j]
        for k in range(line):
            acc = acc + right_mmul(gkv4[s ^ k], ref[k])
        x3[j] = acc
    x = rows[...].T
    scale = rms_scale(x)
    back, term = norm_back(join_lanes(x3, size), x * scale, scale, gain[...])
    result[...] = (grad_mid[...] + back).T
    rows_of = hid3.shape[2]
    lanes = 2 * wide
    each = x.shape[1] // lanes
    for ref, core, m, j in blocks(near, far):
        out = outs[core * chips + m]
        for k in range(line):
            span = slice(k * rows_of, (k + 1) * rows_of)
            out[span] = left_mmul(hid3[j], gkv4[s ^ k]).astype(BF)
        base_row = line * rows_of
        out[base_row:] = jnp.zeros((out.shape[0] - base_row, lanes), BF)
        for n, value in enumerate((term, feed_term[...])):
            for i in range(each):
                at = base_row + n * each + i
                out[at : at + 1] = value[:, i * lanes : (i + 1) * lanes].astype(BF)


def join_kernel(key, value, query, output, out):
    a = key.shape[0]
    b = query.shape[1]
    out[:, :a] = key[...].T
    out[:, a : 2 * a] = value[...].T
    out[:, 2 * a : 2 * a + b] = query[...]
    out[:, 2 * a + b :] = output[...]


def stack_kernel(line, *refs):
    slots, kv, qo = take(refs, line, None, None)
    a = kv.shape[2]
    b = qo.shape[3]
    for k in range(line):
        kv[k] = slots[k][:, :a]
        qo[k, 0] = slots[k][:, a : a + b]
        qo[k, 1] = slots[k][:, a + b :]


def cast_kernel(grad, out):
    out[...] = grad[...].T.astype(BF)


def spread_kernel(gate, up, down, out):
    units = out.shape[2]
    for j in range(out.shape[0]):
        span = slice(j * units, (j + 1) * units)
        out[j, 0] = gate[:, span].T
        out[j, 1] = up[:, span].T
        out[j, 2] = down[:, span].T


def arrange_kernel(got, out):
    cut = got.shape[3]
    units = got.shape[2]
    for j in range(got.shape[0]):
        for n in range(3):
            out[n * units : (n + 1) * units, j * cut : (j + 1) * cut] = got[j, n]


def pair_sum_kernel(chips, *refs):
    near, got, own, outs = take(refs, chips, chips, None, chips - 1)
    own[...] = near[0][...].astype(F32) + got[0][...].astype(F32)
    for m in range(1, chips):
        outs[m - 1][...] = (near[m][...].astype(F32) + got[m][...].astype(F32)).astype(BF)


def stack_sum_kernel(chips, near, *refs):
    got, own, outs = take(refs, chips, None, chips - 1)
    rows = own.shape[0]
    own[...] = near[:rows].astype(F32) + got[0][...].astype(F32)
    for m in range(1, chips):
        mine = near[m * rows : (m + 1) * rows].astype(F32)
        outs[m - 1][...] = (mine + got[m][...].astype(F32)).astype(BF)


def down_end_kernel(mid, own, *refs):
    *got, out = refs
    out[...] = (mid[...] + tree([own[...]] + [g[...].astype(F32) for g in got])).T


def feed_end_kernel(own, *refs):
    *got, out = refs
    whole = tree([own[...]] + [g[...].astype(F32) for g in got]).astype(BF)
    split_lanes(out, whole, out.shape[0])


def feed_done_kernel(got, gate, up, down):
    units = got.shape[2]
    for j in range(got.shape[0]):
        span = slice(j * units, (j + 1) * units)
        gate[:, span] = got[j, 0].astype(F32).T
        up[:, span] = got[j, 1].astype(F32).T
        down[:, span] = got[j, 2].astype(F32).T


def qo_line_kernel(chips, own, *refs):
    got, mine, sent = take(refs, chips - 1, None, len(refs) - chips)
    for k in range(own.shape[0]):
        whole = tree([own[k]] + [g[k].astype(F32) for g in got])
        if k == 0:
            mine[...] = whole
        else:
            sent[k - 1][...] = whole.astype(BF)


def qo_end_kernel(own, *refs):
    *got, query, output = refs
    query[...] = tree([own[0]] + [g[0].astype(F32) for g in got])
    output[...] = tree([own[1]] + [g[1].astype(F32) for g in got])


def kv_line_kernel(chips, line, own, *refs):
    got, mine, gains, sent = take(refs, chips - 1, None, None, line - 1)
    cut = mine.shape[0]
    last = slice(line * cut, None)
    term = tree([own[last].astype(BF).astype(F32)] + [g[last].astype(F32) for g in got]).astype(BF)
    gains[...] = term.astype(F32)
    for k in range(line):
        span = slice(k * cut, (k + 1) * cut)
        whole = tree([own[span]] + [g[span].astype(F32) for g in got])
        if k == 0:
            mine[...] = whole
        else:
            sent[k - 1][:cut] = whole.astype(BF)
            sent[k - 1][cut:] = term


def kv_end_kernel(line, own, own_gains, *refs):
    got, keys, values, attn_gain, feed_gain = take(refs, line - 1, *[None] * 4)
    cut, lanes = own.shape
    whole = tree([own[...]] + [g[:cut].astype(F32) for g in got])
    keys[...] = whole[:, : lanes // 2].T
    values[...] = whole[:, lanes // 2 :].T
    gains = tree([own_gains[...]] + [g[cut:].astype(F32) for g in got])
    each = attn_gain.shape[1] // lanes
    for n, out in enumerate((attn_gain, feed_gain)):
        for i in range(each):
            out[:, i * lanes : (i + 1) * lanes] = gains[n * each + i : n * each + i + 1]


def padded(a):
    if len(a.shape) < 2:
        return 4096
    size = jnp.dtype(a.dtype).itemsize
    *outer, rows, lanes = a.shape
    tile = 32 // size
    return math.prod(outer) * (-(-rows // tile) * tile) * (-(-lanes // 128) * 128) * size


def call(kernel, outs, scratch, flops, *args, far=0, far_outs=(), room=None):
    sizes = [a.size * a.dtype.itemsize for a in (*args, *outs)]
    vmem = pl.BlockSpec(memory_space=pltpu.VMEM)
    free = pl.BlockSpec(memory_space=pl.ANY)
    limit = None
    if room is not None:
        limit = sum(padded(a) for a in (*args, *outs)) + room * 2**20
    return pl.pallas_call(
        kernel,
        out_shape=outs,
        in_specs=[free if i < far else vmem for i in range(len(args))],
        out_specs=[free if i in far_outs else vmem for i in range(len(outs))],
        scratch_shapes=[x if not isinstance(x, tuple) else pltpu.VMEM(x[0], x[1]) for x in scratch],
        cost_estimate=pl.CostEstimate(
            flops=int(flops), bytes_accessed=sum(sizes), transcendentals=0
        ),
        compiler_params=pltpu.CompilerParams(vmem_limit_bytes=limit),
    )(*args)


def array(shape, dtype):
    return jax.ShapeDtypeStruct(shape, dtype)


def flip(x, bits):
    n = lax.axis_size("batch")
    return lax.ppermute(x, "batch", [(i, i ^ bits) for i in range(n)])


def cross(x, bits):
    n = lax.axis_size("seq")
    return lax.ppermute(x, "seq", [(i, i ^ bits) for i in range(n)])


def push(x, by):
    n = lax.axis_size("seq")
    pairs = [(i, i + by) for i in range(n) if 0 <= i + by < n]
    return lax.ppermute(x, "seq", pairs)


def tree(terms):
    while len(terms) > 1:
        terms = [terms[i] + terms[i + 1] for i in range(0, len(terms), 2)]
    return terms[0]


def plane_hops(x, chips):
    return [x] + [flip(x, 2 * m) for m in range(1, chips)]


def pair_swap(xs):
    return [flip(x, 1) for x in xs]


def plane_sum(near, far, chips):
    got = pair_swap(far)
    block = far[0].shape
    one = not isinstance(near, (list, tuple))
    own, *low = call(
        functools.partial(stack_sum_kernel if one else pair_sum_kernel, chips),
        [array(block, F32)] + [array(block, BF)] * (chips - 1),
        [],
        1e6,
        *([near] if one else near),
        *got,
    )
    return own, [flip(low[m - 1], 2 * m) for m in range(1, chips)]


def line_chain(x, line):
    out = []
    for by in (1, -1):
        held = x
        got = []
        for k in range(1, line):
            held = step(held, by, k)
            got.append(held)
        out.append(got)
    return out


def step(x, by, k):
    n = lax.axis_size("seq")
    senders = range(k - 1, n - 1) if by > 0 else range(1, n - k + 1)
    return lax.ppermute(x, "seq", [(i, i + by) for i in senders])


def shards(
    activations,
    segment_ids,
    attention_gain,
    query_weight,
    key_weight,
    value_weight,
    output_weight,
    feed_gain,
    gate_weight,
    up_weight,
    down_weight,
    out_grad,
):
    piece, width = activations.shape[1:]
    line = lax.axis_size("seq")
    size = lax.axis_size("batch")
    length = piece * line
    chips = size // 2
    cut = width // size
    rows = activations[0].T
    grad_rows = out_grad[0].T
    s = lax.axis_index("seq")
    positions = s * piece + jnp.arange(piece, dtype=jnp.int32)
    cosine, sine = rotary_tables(positions.astype(F32))
    gain_attn = attention_gain[None]
    gain_feed = feed_gain[None]
    units = gate_weight.shape[1] // size
    others = range(1, line)

    kv_cols = 2 * key_weight.shape[1]
    qo_cols = query_weight.shape[1]
    (own,) = call(
        join_kernel,
        [array((cut, kv_cols + 2 * qo_cols), BF)],
        [],
        1e5,
        key_weight.T,
        value_weight.T,
        query_weight,
        output_weight,
    )
    kv_slots, qo_slots = call(
        functools.partial(stack_kernel, line),
        [array((line, cut, kv_cols), BF), array((line, 2, cut, qo_cols), BF)],
        [],
        1e5,
        own,
        *[cross(own, k) for k in others],
        room=ROOM,
    )
    kv_near = plane_hops(kv_slots, chips)
    kv_far = pair_swap(kv_near)
    qo_near = plane_hops(qo_slots, chips)
    qo_far = pair_swap(qo_near)

    (local,) = call(
        spread_kernel,
        [array((size, 3, units, cut), BF)],
        [],
        1e5,
        gate_weight,
        up_weight,
        down_weight.T,
    )
    spread = lax.all_to_all(local, "batch", split_axis=0, concat_axis=0, tiled=True)
    (feed_own,) = call(arrange_kernel, [array((3 * units, width), BF)], [], 1e5, spread, room=ROOM)
    feed_right, feed_left = line_chain(feed_own, line)

    (low,) = call(cast_kernel, [array((piece, width), BF)], [], 1e5, grad_rows)
    low_near = plane_hops(low, chips)
    low_far = pair_swap(low_near)

    hidden_attn, packet = call(
        functools.partial(kv_kernel, chips),
        [array((piece, width), BF), array((piece + 8, 2 * KV_WIDTH), BF)],
        [((size, piece, cut), BF), ((line, piece, kv_cols), F32)],
        2 * piece * width * 2 * KV_WIDTH,
        rows,
        gain_attn,
        cosine,
        sine,
        segment_ids,
        *kv_near,
        *kv_far,
    )
    packets = [packet] + [push(packet, k) for k in others]
    (query,) = call(
        functools.partial(query_kernel, chips),
        [array((piece, width), BF)],
        [((size, piece, cut), BF), ((line, piece, qo_cols), F32)],
        2 * piece * width * width,
        hidden_attn,
        cosine,
        sine,
        *qo_near,
        *qo_far,
    )
    probs, attn, mid, hidden_feed = call(
        functools.partial(attention_kernel, chips, line),
        [
            array((KV_HEADS, GROUPS * piece, length), F32),
            array((piece, width), BF),
            array((piece, width), F32),
            array((piece, width), BF),
        ],
        [((piece, length), F32), ((size, piece, cut), BF), ((line, piece, qo_cols), F32)],
        2 * piece * width * (width + 2 * length),
        query,
        *packets,
        rows,
        segment_ids,
        gain_feed,
        *qo_near,
        *qo_far,
    )
    hid_near = plane_hops(hidden_feed, chips)
    hid_far = pair_swap(hid_near)
    flat = (chips * piece, width)
    tokens = size * piece
    act = (tokens, line * units)
    feed_in = [*hid_near, *hid_far, *low_near, *low_far, feed_own, *feed_right, *feed_left]
    slots = [((line, 3 * units, width), BF), ((line * units, width), BF)]
    both = [((tokens, width), BF)] * 2
    sems = pltpu.SemaphoreType.DMA((4 * chips,))
    back_near, *rest = call(
        functools.partial(feed_kernel, chips, line, 2 * piece),
        [array(flat, BF)] + [array((piece, width), BF)] * chips + [array(act, BF)] * 3,
        [
            slots[0],
            slots[1],
            slots[1],
            slots[1],
            *both,
            (flat, BF),
            sems,
            pltpu.SemaphoreType.DMA((chips,)),
        ],
        10 * tokens * width * line * units,
        *feed_in,
        far=len(feed_in),
        far_outs=range(1, chips + 1),
    )
    back_far, acts = rest[:chips], rest[chips:]
    back_own, back_got = plane_sum(back_near, back_far, chips)
    down_near, *rest = call(
        functools.partial(feed_grad_kernel, chips, line),
        [array(flat, BF)]
        + [array((piece, width), BF)] * chips
        + [array((3 * units, width), F32)]
        + [array((3 * units, width), BF)] * (line - 1),
        [*slots, *both, sems],
        8 * tokens * width * line * units,
        *feed_in,
        *acts,
        far=len(feed_in),
    )
    down_far, feed_grads = rest[:chips], rest[chips:]
    grad_mid, feed_term, grad_mid_low, grad_query, kv_own, *kv_sent = call(
        functools.partial(middle_kernel, chips, line),
        [
            array((piece, width), F32),
            array((1, width), F32),
            array((piece, width), BF),
            array((piece, width), BF),
            array((piece, 2 * KV_WIDTH), F32),
        ]
        + [array((piece, 2 * KV_WIDTH), BF)] * (line - 1),
        [
            ((line, piece, qo_cols), BF),
            ((size, piece, cut), BF),
            ((piece, width), BF),
            ((length, 2 * KV_WIDTH), F32),
        ],
        2 * piece * width * (width + 4 * length),
        back_own,
        *back_got,
        mid,
        grad_rows,
        gain_feed,
        attn,
        query,
        probs,
        cosine,
        sine,
        *qo_near,
        *qo_far,
        *packets,
    )
    kv_got = [push(kv_sent[k - 1], -k) for k in others]

    down_own, down_got = plane_sum(down_near, down_far, chips)
    (block_output,) = call(
        down_end_kernel, [array((width, piece), F32)], [], 1e6, mid, down_own, *down_got, room=ROOM
    )

    feed_got = [cross(feed_grads[k], k) for k in others]
    (feed_own,) = call(
        feed_end_kernel,
        [array((size, 3 * units, cut), BF)],
        [],
        1e6,
        feed_grads[0],
        *feed_got,
        room=ROOM,
    )
    feed_back = lax.all_to_all(feed_own, "batch", split_axis=0, concat_axis=0, tiled=True)
    gate_done, up_done, down_done = call(
        feed_done_kernel,
        [
            array(gate_weight.shape, F32),
            array(up_weight.shape, F32),
            array(down_weight.shape[::-1], F32),
        ],
        [],
        1e6,
        feed_back.reshape(size, 3, units, cut),
        room=ROOM,
    )

    shape = (line, 2, cut, qo_cols)
    *qo_grads, base = call(
        functools.partial(query_grad_kernel, chips),
        [array(shape, BF)] * size + [array((size, piece, cut), F32)],
        [((size, piece, cut), BF)] * 2 + [((line, piece, qo_cols), BF)] * 2,
        6 * piece * width * width,
        hidden_attn,
        grad_query,
        attn,
        grad_mid_low,
        *qo_near,
        *qo_far,
    )
    qo_own, qo_got = plane_sum(qo_grads[:chips], qo_grads[chips:], chips)
    block = (2, cut, qo_cols)
    qo_own, *qo_sent = call(
        functools.partial(qo_line_kernel, chips),
        [array(block, F32)] + [array(block, BF)] * (line - 1),
        [],
        1e6,
        qo_own,
        *qo_got,
        room=ROOM,
    )
    qo_got = [cross(qo_sent[k - 1], k) for k in others]
    query_done, output_done = call(
        qo_end_kernel, [array((cut, qo_cols), F32)] * 2, [], 1e6, qo_own, *qo_got, room=ROOM
    )

    each = width // kv_cols
    extra = -(-2 * each // 16) * 16
    shape = (line * cut + extra, kv_cols)
    input_grad, *kv_grads = call(
        functools.partial(input_grad_kernel, chips, line),
        [array((width, piece), F32)] + [array(shape, BF)] * size,
        [
            ((size, piece, cut), BF),
            ((piece, 2 * KV_WIDTH), BF),
            ((line, piece, kv_cols), BF),
            ((size, piece, cut), F32),
        ],
        4 * piece * width * 2 * KV_WIDTH,
        kv_own,
        *kv_got,
        rows,
        gain_attn,
        hidden_attn,
        grad_mid,
        base,
        cosine,
        sine,
        feed_term,
        *kv_near,
        *kv_far,
    )
    kv_own, kv_got = plane_sum(kv_grads[:chips], kv_grads[chips:], chips)
    kv_own, own_gains, *kv_sent = call(
        functools.partial(kv_line_kernel, chips, line),
        [array((cut, kv_cols), F32), array((extra, kv_cols), F32)]
        + [array((cut + extra, kv_cols), BF)] * (line - 1),
        [],
        1e6,
        kv_own,
        *kv_got,
        room=ROOM,
    )
    kv_got = [cross(kv_sent[k - 1], k) for k in others]
    key_done, value_done, attn_gain_sum, feed_gain_sum = call(
        functools.partial(kv_end_kernel, line),
        [array((kv_cols // 2, cut), F32)] * 2 + [array((1, width), F32)] * 2,
        [],
        1e6,
        kv_own,
        own_gains,
        *kv_got,
        room=ROOM,
    )
    return (
        block_output.T[None],
        input_grad.T[None],
        attn_gain_sum[0],
        query_done,
        key_done.T,
        value_done.T,
        output_done,
        feed_gain_sum[0],
        gate_done,
        up_done,
        down_done.T,
    )


def solution(mesh):
    both = P("batch", "seq")
    tokens = P("batch", "seq", None)
    in_specs = (tokens, both, P(), both, both, both, both, P(), both, both, P("seq", "batch"), tokens)
    out_specs = (tokens, tokens, P(), both, both, both, both, P(), both, both, P("seq", "batch"))

    return jax.shard_map(shards, mesh=mesh, in_specs=in_specs, out_specs=out_specs, check_vma=False)
```

```python
import functools
import math

import jax
import jax.numpy as jnp
from jax import lax
from jax.experimental import pallas as pl
from jax.experimental.pallas import tpu as pltpu
from jax.sharding import PartitionSpec as P


HEADS = 15
KV_HEADS = 5
HEAD_DIM = 64
GROUPS = HEADS // KV_HEADS
KV_WIDTH = KV_HEADS * HEAD_DIM
HALF = HEAD_DIM // 2
INV_ROOT = 1.0 / HEAD_DIM**0.5
BF = jnp.bfloat16
F32 = jnp.float32
ROOM = 6


def rotary_tables(positions):
    expon = jnp.arange(HALF, dtype=F32) * (2.0 / HEAD_DIM)
    inverse = jnp.power(F32(10000.0), -expon)
    angles = positions[:, None] * inverse[None, :]
    return jnp.cos(angles), jnp.sin(angles)


def mmul(left, right):
    return jnp.dot(left, right, preferred_element_type=F32)


def left_mmul(left, right):
    return lax.dot_general(left, right, (((0,), (0,)), ((), ())), preferred_element_type=F32)


def right_mmul(left, right):
    return lax.dot_general(left, right, (((1,), (1,)), ((), ())), preferred_element_type=F32)


def head_of(h):
    return slice(h * HEAD_DIM, (h + 1) * HEAD_DIM)


def tables(cosine, sine):
    c, d = cosine[...], sine[...]
    return jnp.concatenate([c, c], 1), jnp.concatenate([-d, d], 1)


def swapped(x):
    return jnp.concatenate([x[:, HALF:], x[:, :HALF]], 1)


def rms_scale(rows):
    return lax.rsqrt(jnp.mean(rows * rows, -1, keepdims=True) + 1e-05)


def norm_back(grad_out, normed, scale, gain):
    scaled = grad_out * gain
    inner = jnp.mean(scaled * normed, -1, keepdims=True)
    return (scale * (scaled - normed * inner), jnp.sum(grad_out * normed, 0, keepdims=True))


def split_lanes(ref, value, count):
    wide = value.shape[1] // count
    for j in range(count):
        ref[j] = value[:, j * wide : (j + 1) * wide]


def join_lanes(ref, count):
    return jnp.concatenate([ref[j] for j in range(count)], 1)


def blocks(near, far):
    b = lax.axis_index("batch")
    out = []
    for core, refs in ((0, near), (1, far)):
        for m, ref in enumerate(refs):
            out.append((ref, core, m, b ^ (2 * m + core)))
    return out


def take(refs, *counts):
    out = []
    at = 0
    for n in counts:
        out.append(refs[at] if n is None else refs[at : at + n])
        at += 1 if n is None else n
    assert at == len(refs)
    return out


def kv_kernel(chips, *refs):
    rows, gain, cosine, sine, seg, near, far, hidden, packet, hid3, acc4 = take(
        refs, *[None] * 5, chips, chips, *[None] * 4
    )
    line = near[0].shape[0]
    s = lax.axis_index("seq")
    piece = rows.shape[1]
    cos, sin = tables(cosine, sine)
    x = rows[...].T
    hid = (x * rms_scale(x) * gain[...]).astype(BF)
    hidden[...] = hid
    split_lanes(hid3, hid, hid3.shape[0])
    for k in range(line):
        acc = 0.0
        for ref, _, m, at in blocks(near, far):
            acc = acc + mmul(hid3[at], ref[k])
        acc4[s ^ k] = acc
    wide = near[0].shape[-1] // 2
    keys = jnp.concatenate([acc4[p, :, :wide] for p in range(line)], 1)
    values = jnp.concatenate([acc4[p, :, wide:] for p in range(line)], 1)
    for h in range(KV_HEADS):
        u = keys[:, head_of(h)]
        packet[:piece, head_of(h)] = (u * cos + swapped(u) * sin).astype(BF)
    packet[:piece, KV_WIDTH:] = values.astype(BF)
    packet[piece:, :] = jnp.zeros((packet.shape[0] - piece, packet.shape[1]), BF)
    packet[piece:, :piece] = jnp.broadcast_to(
        seg[...].astype(F32), (packet.shape[0] - piece, piece)
    ).astype(BF)


def query_kernel(chips, *refs):
    hidden, cosine, sine, near, far, query, hid3, acc4 = take(
        refs, None, None, None, chips, chips, None, None, None
    )
    line = near[0].shape[0]
    s = lax.axis_index("seq")
    cos, sin = tables(cosine, sine)
    split_lanes(hid3, hidden[...], hid3.shape[0])
    for k in range(line):
        acc = 0.0
        for ref, _, m, at in blocks(near, far):
            acc = acc + mmul(hid3[at], ref[k, 0])
        acc4[s ^ k] = acc
    full = join_lanes(acc4, line)
    for h in range(HEADS):
        u = full[:, head_of(h)]
        query[:, head_of(h)] = (u * cos + swapped(u) * sin).astype(BF)


def group_rows(ref, g):
    return jnp.concatenate([ref[:, head_of(GROUPS * g + i)] for i in range(GROUPS)], 0)


def slot_rows(packets, piece, lanes):
    return jnp.concatenate([p[:piece, lanes] for p in packets], 0)


def attention_kernel(chips, line, *refs):
    query, packets, rows, seg, gain, near, far, *rest = take(
        refs, None, line, None, None, None, chips, chips, *[None] * 7
    )
    probs, attn, mid, hidden, bias, att3, acc4 = rest
    s = lax.axis_index("seq")
    piece = rows.shape[1]
    mine = jnp.broadcast_to(seg[...].astype(F32), (piece, piece)).T
    at = lax.broadcasted_iota(jnp.int32, (piece, piece), 0)
    key = lax.broadcasted_iota(jnp.int32, (piece, piece), 1)
    for k in range(line):
        same = mine == packets[k][piece : piece + 1, :piece].astype(F32)
        ok = same & (key - k * piece <= at) & (key + (s - k) * piece >= 0)
        bias[:, k * piece : (k + 1) * piece] = jnp.where(ok, 0.0, -jnp.inf)
    for g in range(KV_HEADS):
        keys = slot_rows(packets, piece, head_of(g))
        values = slot_rows(packets, piece, head_of(KV_HEADS + g))
        scores = right_mmul(group_rows(query, g), keys) * INV_ROOT
        scores = scores + jnp.concatenate([bias[...]] * GROUPS, 0)
        raised = jnp.exp(scores - jnp.max(scores, -1, keepdims=True))
        weights = raised / jnp.sum(raised, -1, keepdims=True)
        probs[g] = weights
        out = mmul(weights.astype(BF), values).astype(BF)
        for i in range(GROUPS):
            attn[:, head_of(GROUPS * g + i)] = out[i * piece : (i + 1) * piece]
    split_lanes(att3, attn[...], att3.shape[0])
    for k in range(line):
        acc = 0.0
        for ref, _, m, j in blocks(near, far):
            acc = acc + mmul(att3[j], ref[k, 1])
        acc4[s ^ k] = acc
    x = rows[...].T + join_lanes(acc4, line)
    mid[...] = x
    hidden[...] = (x * rms_scale(x) * gain[...]).astype(BF)


def load_all(refs, scratch, sems):
    rows = refs[0].shape[0]
    copies = [
        pltpu.make_async_copy(ref, scratch.at[pl.ds(i * rows, rows)], sems.at[i])
        for i, ref in enumerate(refs)
    ]
    for copy in copies:
        copy.start()
    return copies


def load_slots(own, right, left, slots):
    s = lax.axis_index("seq")
    line = slots.shape[0]
    pltpu.sync_copy(own, slots.at[0])
    for k in range(1, line):
        for far in range(1, line):

            @pl.when((s ^ k) == s - far)
            def _():
                pltpu.sync_copy(right[far - 1], slots.at[k])

            @pl.when((s ^ k) == s + far)
            def _():
                pltpu.sync_copy(left[far - 1], slots.at[k])


def feed_kernel(chips, line, tile, *refs):
    hid, low, own, right, left, back_near, back_far, gate_s, up_s, inner_s, *scratch = take(
        refs, 2 * chips, 2 * chips, None, line - 1, line - 1, None, chips, *[None] * 12
    )
    slots, gate_w, up_w, down_w, hid_s, low_s, far_s, sems, far_sems = scratch
    copies = load_all(hid, hid_s, sems) + load_all(low, low_s, sems.at[pl.ds(2 * chips, 2 * chips)])
    load_slots(own, right, left, slots)
    piece = hid[0].shape[0]
    units = own.shape[0] // 3
    for k in range(line):
        span = slice(k * units, (k + 1) * units)
        gate_w[span] = slots[k, :units]
        up_w[span] = slots[k, units : 2 * units]
        down_w[span] = slots[k, 2 * units :]
    for copy in copies:
        copy.wait()
    half = chips * piece

    def run(back, base):
        def body(i, carry):
            span = pl.ds(pl.multiple_of(i * tile, tile), tile)
            read = pl.ds(pl.multiple_of(base + i * tile, tile), tile)
            h = hid_s[read]
            gate = right_mmul(h, gate_w[...])
            up = right_mmul(h, up_w[...])
            inner_grad = right_mmul(low_s[read], down_w[...])
            sigma = jax.nn.sigmoid(gate)
            inner_s[read] = (gate * sigma * up).astype(BF)
            grad_up = (inner_grad * gate * sigma).astype(BF)
            grad_gate = (inner_grad * up * sigma * (1.0 + gate * (1.0 - sigma))).astype(BF)
            gate_s[read] = grad_gate
            up_s[read] = grad_up
            total_back = mmul(grad_gate, gate_w[...]) + mmul(grad_up, up_w[...])
            back[span] = total_back.astype(BF)
            return carry

        lax.fori_loop(0, half // tile, body, 0)

    run(far_s, half)
    sends = [
        pltpu.make_async_copy(far_s.at[pl.ds(m * piece, piece)], back_far[m], far_sems.at[m])
        for m in range(chips)
    ]
    for send in sends:
        send.start()
    run(back_near, 0)
    for send in sends:
        send.wait()


def feed_grad_kernel(chips, line, *refs):
    hid, low, own, right, left, gate_s, up_s, inner_s, down_near, down_far, grads, *scratch = take(
        refs, 2 * chips, 2 * chips, None, line - 1, line - 1, *[None] * 4, chips, line, *[None] * 5
    )
    slots, down_w, hid_s, low_s, sems = scratch
    copies = load_all(hid, hid_s, sems) + load_all(low, low_s, sems.at[pl.ds(2 * chips, 2 * chips)])
    load_slots(own, right, left, slots)
    piece = hid[0].shape[0]
    units = own.shape[0] // 3
    for k in range(line):
        down_w[k * units : (k + 1) * units] = slots[k, 2 * units :]
    for copy in copies:
        copy.wait()
    half = chips * piece
    for m in range(chips):
        span = slice(m * piece, (m + 1) * piece)
        far = slice(half + m * piece, half + (m + 1) * piece)
        down_near[span] = mmul(inner_s[span], down_w[...]).astype(BF)
        down_far[m][...] = mmul(inner_s[far], down_w[...]).astype(BF)
    for n, (a, b) in enumerate(((gate_s, hid_s), (up_s, hid_s), (inner_s, low_s))):
        term = left_mmul(a[...], b[...])
        for k in range(line):
            out = term[k * units : (k + 1) * units]
            grads[k][n * units : (n + 1) * units] = out.astype(grads[k].dtype)


def middle_kernel(chips, line, *refs):
    parts, mid, out_grad, gain, attn, query, probs, cosine, sine, near, far, packets, *rest = take(
        refs, chips, *[None] * 8, chips, chips, line, *[None] * 4, line, *[None] * 4
    )
    grad_mid, gain_term, grad_low, grad_query, slots, low4, att3, grad_attn, grad_kv = rest
    s = lax.axis_index("seq")
    piece = mid.shape[0]
    cos, sin = tables(cosine, sine)
    grad = parts[0][...].astype(F32)
    for part in parts[1:]:
        grad = grad + part[...].astype(F32)
    x = mid[...]
    scale = rms_scale(x)
    back, term = norm_back(grad, x * scale, scale, gain[...])
    gain_term[...] = term
    whole = out_grad[...].T + back
    grad_mid[...] = whole
    low = whole.astype(BF)
    grad_low[...] = low
    split_lanes(low4, low, line)
    for ref, _, m, j in blocks(near, far):
        acc = 0.0
        for k in range(line):
            acc = acc + right_mmul(low4[s ^ k], ref[k, 1])
        att3[j] = acc.astype(BF)
    grad_attn[...] = join_lanes(att3, att3.shape[0])
    for g in range(KV_HEADS):
        keys = slot_rows(packets, piece, head_of(g))
        values = slot_rows(packets, piece, head_of(KV_HEADS + g))
        q = group_rows(query, g)
        ga = group_rows(grad_attn, g)
        at = group_rows(attn, g)
        dots = jnp.sum(ga.astype(F32) * at.astype(F32), -1, keepdims=True)
        weights = probs[g]
        gs = (weights * (right_mmul(ga, values) - dots) * INV_ROOT).astype(BF)
        gq = mmul(gs, keys)
        for i in range(GROUPS):
            u = gq[i * piece : (i + 1) * piece]
            h = GROUPS * g + i
            grad_query[:, head_of(h)] = (u * cos - swapped(u) * sin).astype(BF)
        grad_kv[:, head_of(g)] = left_mmul(gs, q)
        grad_kv[:, head_of(KV_HEADS + g)] = left_mmul(weights.astype(BF), ga)
    for k in range(line):
        slots[k][...] = grad_kv[k * piece : (k + 1) * piece].astype(slots[k].dtype)


def query_grad_kernel(chips, *refs):
    hidden, grad_query, attn, grad_low, near, far, out_near, out_far, back, *scratch = take(
        refs, *[None] * 4, chips, chips, chips, chips, *[None] * 5
    )
    hid3, att3, gq4, low4 = scratch
    line = near[0].shape[0]
    s = lax.axis_index("seq")
    size = hid3.shape[0]
    split_lanes(hid3, hidden[...], size)
    split_lanes(att3, attn[...], size)
    split_lanes(gq4, grad_query[...], line)
    split_lanes(low4, grad_low[...], line)
    for ref, core, m, j in blocks(near, far):
        out = (out_near, out_far)[core][m]
        for k in range(line):
            out[k, 0] = left_mmul(hid3[j], gq4[s ^ k]).astype(BF)
            out[k, 1] = left_mmul(att3[j], low4[s ^ k]).astype(BF)
    for ref, _, m, j in blocks(near, far):
        acc = 0.0
        for k in range(line):
            acc = acc + right_mmul(gq4[s ^ k], ref[k, 0])
        back[j] = acc


def input_grad_kernel(chips, line, *refs):
    parts, rows, gain, hidden, grad_mid, base, cosine, sine, feed_term, near, far, *rest = take(
        refs, line, *[None] * 8, chips, chips, None, 2 * chips, *[None] * 4
    )
    result, outs, hid3, full, gkv4, x3 = take(rest, *[None] * 6)
    cos, sin = tables(cosine, sine)
    s = lax.axis_index("seq")
    size = hid3.shape[0]
    both = parts[0][...]
    for part in parts[1:]:
        both = both + part[...].astype(F32)
    for h in range(KV_HEADS):
        u = both[:, head_of(h)]
        full[:, head_of(h)] = (u * cos - swapped(u) * sin).astype(BF)
    full[:, KV_WIDTH:] = both[:, KV_WIDTH:].astype(BF)
    wide = KV_WIDTH // line
    for p in range(line):
        gkv4[p, :, :wide] = full[:, p * wide : (p + 1) * wide]
        gkv4[p, :, wide:] = full[:, KV_WIDTH + p * wide : KV_WIDTH + (p + 1) * wide]
    split_lanes(hid3, hidden[...], size)
    for ref, _, m, j in blocks(near, far):
        acc = base[j]
        for k in range(line):
            acc = acc + right_mmul(gkv4[s ^ k], ref[k])
        x3[j] = acc
    x = rows[...].T
    scale = rms_scale(x)
    back, term = norm_back(join_lanes(x3, size), x * scale, scale, gain[...])
    result[...] = (grad_mid[...] + back).T
    rows_of = hid3.shape[2]
    lanes = 2 * wide
    each = x.shape[1] // lanes
    for ref, core, m, j in blocks(near, far):
        out = outs[core * chips + m]
        for k in range(line):
            span = slice(k * rows_of, (k + 1) * rows_of)
            out[span] = left_mmul(hid3[j], gkv4[s ^ k]).astype(BF)
        base_row = line * rows_of
        out[base_row:] = jnp.zeros((out.shape[0] - base_row, lanes), BF)
        for n, value in enumerate((term, feed_term[...])):
            for i in range(each):
                at = base_row + n * each + i
                out[at : at + 1] = value[:, i * lanes : (i + 1) * lanes].astype(BF)


def join_kernel(key, value, query, output, out):
    a = key.shape[0]
    b = query.shape[1]
    out[:, :a] = key[...].T
    out[:, a : 2 * a] = value[...].T
    out[:, 2 * a : 2 * a + b] = query[...]
    out[:, 2 * a + b :] = output[...]


def stack_kernel(line, *refs):
    slots, kv, qo = take(refs, line, None, None)
    a = kv.shape[2]
    b = qo.shape[3]
    for k in range(line):
        kv[k] = slots[k][:, :a]
        qo[k, 0] = slots[k][:, a : a + b]
        qo[k, 1] = slots[k][:, a + b :]


def cast_kernel(grad, out):
    out[...] = grad[...].T.astype(BF)


def spread_kernel(gate, up, down, out):
    units = out.shape[2]
    for j in range(out.shape[0]):
        span = slice(j * units, (j + 1) * units)
        out[j, 0] = gate[:, span].T
        out[j, 1] = up[:, span].T
        out[j, 2] = down[:, span].T


def arrange_kernel(got, out):
    cut = got.shape[3]
    units = got.shape[2]
    for j in range(got.shape[0]):
        for n in range(3):
            out[n * units : (n + 1) * units, j * cut : (j + 1) * cut] = got[j, n]


def pair_sum_kernel(chips, *refs):
    near, got, own, outs = take(refs, chips, chips, None, chips - 1)
    own[...] = near[0][...].astype(F32) + got[0][...].astype(F32)
    for m in range(1, chips):
        outs[m - 1][...] = (near[m][...].astype(F32) + got[m][...].astype(F32)).astype(BF)


def stack_sum_kernel(chips, near, *refs):
    got, own, outs = take(refs, chips, None, chips - 1)
    rows = own.shape[0]
    own[...] = near[:rows].astype(F32) + got[0][...].astype(F32)
    for m in range(1, chips):
        mine = near[m * rows : (m + 1) * rows].astype(F32)
        outs[m - 1][...] = (mine + got[m][...].astype(F32)).astype(BF)


def down_end_kernel(mid, own, *refs):
    *got, out = refs
    out[...] = (mid[...] + tree([own[...]] + [g[...].astype(F32) for g in got])).T


def feed_end_kernel(own, *refs):
    *got, out = refs
    whole = tree([own[...]] + [g[...].astype(F32) for g in got]).astype(BF)
    split_lanes(out, whole, out.shape[0])


def feed_done_kernel(got, gate, up, down):
    units = got.shape[2]
    for j in range(got.shape[0]):
        span = slice(j * units, (j + 1) * units)
        gate[:, span] = got[j, 0].astype(F32).T
        up[:, span] = got[j, 1].astype(F32).T
        down[:, span] = got[j, 2].astype(F32).T


def qo_line_kernel(chips, own, *refs):
    got, mine, sent = take(refs, chips - 1, None, len(refs) - chips)
    for k in range(own.shape[0]):
        whole = tree([own[k]] + [g[k].astype(F32) for g in got])
        if k == 0:
            mine[...] = whole
        else:
            sent[k - 1][...] = whole.astype(BF)


def qo_end_kernel(own, *refs):
    *got, query, output = refs
    query[...] = tree([own[0]] + [g[0].astype(F32) for g in got])
    output[...] = tree([own[1]] + [g[1].astype(F32) for g in got])


def kv_line_kernel(chips, line, own, *refs):
    got, mine, gains, sent = take(refs, chips - 1, None, None, line - 1)
    cut = mine.shape[0]
    last = slice(line * cut, None)
    term = tree([own[last].astype(BF).astype(F32)] + [g[last].astype(F32) for g in got]).astype(BF)
    gains[...] = term.astype(F32)
    for k in range(line):
        span = slice(k * cut, (k + 1) * cut)
        whole = tree([own[span]] + [g[span].astype(F32) for g in got])
        if k == 0:
            mine[...] = whole
        else:
            sent[k - 1][:cut] = whole.astype(BF)
            sent[k - 1][cut:] = term


def kv_end_kernel(line, own, own_gains, *refs):
    got, keys, values, attn_gain, feed_gain = take(refs, line - 1, *[None] * 4)
    cut, lanes = own.shape
    whole = tree([own[...]] + [g[:cut].astype(F32) for g in got])
    keys[...] = whole[:, : lanes // 2].T
    values[...] = whole[:, lanes // 2 :].T
    gains = tree([own_gains[...]] + [g[cut:].astype(F32) for g in got])
    each = attn_gain.shape[1] // lanes
    for n, out in enumerate((attn_gain, feed_gain)):
        for i in range(each):
            out[:, i * lanes : (i + 1) * lanes] = gains[n * each + i : n * each + i + 1]


def padded(a):
    if len(a.shape) < 2:
        return 4096
    size = jnp.dtype(a.dtype).itemsize
    *outer, rows, lanes = a.shape
    tile = 32 // size
    return math.prod(outer) * (-(-rows // tile) * tile) * (-(-lanes // 128) * 128) * size


def call(kernel, outs, scratch, flops, *args, far=0, far_outs=()):
    sizes = [a.size * a.dtype.itemsize for a in (*args, *outs)]
    vmem = pl.BlockSpec(memory_space=pltpu.VMEM)
    free = pl.BlockSpec(memory_space=pl.ANY)
    held = [a for i, a in enumerate(args) if i >= far]
    held += [a for i, a in enumerate(outs) if i not in far_outs]
    held += [array(*x) for x in scratch if isinstance(x, tuple)]
    limit = min(sum(padded(a) for a in held) + ROOM * 2**20, 60 * 1024 * 2**10)
    return pl.pallas_call(
        kernel,
        out_shape=outs,
        in_specs=[free if i < far else vmem for i in range(len(args))],
        out_specs=[free if i in far_outs else vmem for i in range(len(outs))],
        scratch_shapes=[x if not isinstance(x, tuple) else pltpu.VMEM(x[0], x[1]) for x in scratch],
        cost_estimate=pl.CostEstimate(
            flops=int(flops), bytes_accessed=sum(sizes), transcendentals=0
        ),
        compiler_params=pltpu.CompilerParams(vmem_limit_bytes=limit),
    )(*args)


def array(shape, dtype):
    return jax.ShapeDtypeStruct(shape, dtype)


def flip(x, bits):
    n = lax.axis_size("batch")
    return lax.ppermute(x, "batch", [(i, i ^ bits) for i in range(n)])


def cross(x, bits):
    n = lax.axis_size("seq")
    return lax.ppermute(x, "seq", [(i, i ^ bits) for i in range(n)])


def push(x, by):
    n = lax.axis_size("seq")
    pairs = [(i, i + by) for i in range(n) if 0 <= i + by < n]
    return lax.ppermute(x, "seq", pairs)


def tree(terms):
    while len(terms) > 1:
        terms = [terms[i] + terms[i + 1] for i in range(0, len(terms), 2)]
    return terms[0]


def plane_hops(x, chips):
    return [x] + [flip(x, 2 * m) for m in range(1, chips)]


def pair_swap(xs):
    return [flip(x, 1) for x in xs]


def plane_sum(near, far, chips):
    got = pair_swap(far)
    block = far[0].shape
    one = not isinstance(near, (list, tuple))
    own, *low = call(
        functools.partial(stack_sum_kernel if one else pair_sum_kernel, chips),
        [array(block, F32)] + [array(block, BF)] * (chips - 1),
        [],
        1e6,
        *([near] if one else near),
        *got,
    )
    return own, [flip(low[m - 1], 2 * m) for m in range(1, chips)]


def line_chain(x, line):
    out = []
    for by in (1, -1):
        held = x
        got = []
        for k in range(1, line):
            held = step(held, by, k)
            got.append(held)
        out.append(got)
    return out


def step(x, by, k):
    n = lax.axis_size("seq")
    senders = range(k - 1, n - 1) if by > 0 else range(1, n - k + 1)
    return lax.ppermute(x, "seq", [(i, i + by) for i in senders])


def shards(
    activations,
    segment_ids,
    attention_gain,
    query_weight,
    key_weight,
    value_weight,
    output_weight,
    feed_gain,
    gate_weight,
    up_weight,
    down_weight,
    out_grad,
):
    piece, width = activations.shape[1:]
    line = lax.axis_size("seq")
    size = lax.axis_size("batch")
    length = piece * line
    chips = size // 2
    cut = width // size
    rows = activations[0].T
    grad_rows = out_grad[0].T
    s = lax.axis_index("seq")
    positions = s * piece + jnp.arange(piece, dtype=jnp.int32)
    cosine, sine = rotary_tables(positions.astype(F32))
    gain_attn = attention_gain[None]
    gain_feed = feed_gain[None]
    units = gate_weight.shape[1] // size
    others = range(1, line)

    kv_cols = 2 * key_weight.shape[1]
    qo_cols = query_weight.shape[1]
    (own,) = call(
        join_kernel,
        [array((cut, kv_cols + 2 * qo_cols), BF)],
        [],
        1e5,
        key_weight.T,
        value_weight.T,
        query_weight,
        output_weight,
    )
    kv_slots, qo_slots = call(
        functools.partial(stack_kernel, line),
        [array((line, cut, kv_cols), BF), array((line, 2, cut, qo_cols), BF)],
        [],
        1e5,
        own,
        *[cross(own, k) for k in others],
    )
    kv_near = plane_hops(kv_slots, chips)
    kv_far = pair_swap(kv_near)
    qo_near = plane_hops(qo_slots, chips)
    qo_far = pair_swap(qo_near)

    (local,) = call(
        spread_kernel,
        [array((size, 3, units, cut), BF)],
        [],
        1e5,
        gate_weight,
        up_weight,
        down_weight.T,
    )
    spread = lax.all_to_all(local, "batch", split_axis=0, concat_axis=0, tiled=True)
    (feed_own,) = call(arrange_kernel, [array((3 * units, width), BF)], [], 1e5, spread)
    feed_right, feed_left = line_chain(feed_own, line)

    (low,) = call(cast_kernel, [array((piece, width), BF)], [], 1e5, grad_rows)
    low_near = plane_hops(low, chips)
    low_far = pair_swap(low_near)

    hidden_attn, packet = call(
        functools.partial(kv_kernel, chips),
        [array((piece, width), BF), array((piece + 8, 2 * KV_WIDTH), BF)],
        [((size, piece, cut), BF), ((line, piece, kv_cols), F32)],
        2 * piece * width * 2 * KV_WIDTH,
        rows,
        gain_attn,
        cosine,
        sine,
        segment_ids,
        *kv_near,
        *kv_far,
    )
    packets = [packet] + [push(packet, k) for k in others]
    (query,) = call(
        functools.partial(query_kernel, chips),
        [array((piece, width), BF)],
        [((size, piece, cut), BF), ((line, piece, qo_cols), F32)],
        2 * piece * width * width,
        hidden_attn,
        cosine,
        sine,
        *qo_near,
        *qo_far,
    )
    probs, attn, mid, hidden_feed = call(
        functools.partial(attention_kernel, chips, line),
        [
            array((KV_HEADS, GROUPS * piece, length), F32),
            array((piece, width), BF),
            array((piece, width), F32),
            array((piece, width), BF),
        ],
        [((piece, length), F32), ((size, piece, cut), BF), ((line, piece, qo_cols), F32)],
        2 * piece * width * (width + 2 * length),
        query,
        *packets,
        rows,
        segment_ids,
        gain_feed,
        *qo_near,
        *qo_far,
    )
    hid_near = plane_hops(hidden_feed, chips)
    hid_far = pair_swap(hid_near)
    flat = (chips * piece, width)
    tokens = size * piece
    act = (tokens, line * units)
    feed_in = [*hid_near, *hid_far, *low_near, *low_far, feed_own, *feed_right, *feed_left]
    slots = [((line, 3 * units, width), BF), ((line * units, width), BF)]
    both = [((tokens, width), BF)] * 2
    sems = pltpu.SemaphoreType.DMA((4 * chips,))
    back_near, *rest = call(
        functools.partial(feed_kernel, chips, line, 2 * piece),
        [array(flat, BF)] + [array((piece, width), BF)] * chips + [array(act, BF)] * 3,
        [
            slots[0],
            slots[1],
            slots[1],
            slots[1],
            *both,
            (flat, BF),
            sems,
            pltpu.SemaphoreType.DMA((chips,)),
        ],
        10 * tokens * width * line * units,
        *feed_in,
        far=len(feed_in),
        far_outs=range(1, chips + 1),
    )
    back_far, acts = rest[:chips], rest[chips:]
    back_own, back_got = plane_sum(back_near, back_far, chips)
    down_near, *rest = call(
        functools.partial(feed_grad_kernel, chips, line),
        [array(flat, BF)]
        + [array((piece, width), BF)] * chips
        + [array((3 * units, width), F32)]
        + [array((3 * units, width), BF)] * (line - 1),
        [*slots, *both, sems],
        8 * tokens * width * line * units,
        *feed_in,
        *acts,
        far=len(feed_in),
    )
    down_far, feed_grads = rest[:chips], rest[chips:]
    grad_mid, feed_term, grad_mid_low, grad_query, kv_own, *kv_sent = call(
        functools.partial(middle_kernel, chips, line),
        [
            array((piece, width), F32),
            array((1, width), F32),
            array((piece, width), BF),
            array((piece, width), BF),
            array((piece, 2 * KV_WIDTH), F32),
        ]
        + [array((piece, 2 * KV_WIDTH), BF)] * (line - 1),
        [
            ((line, piece, qo_cols), BF),
            ((size, piece, cut), BF),
            ((piece, width), BF),
            ((length, 2 * KV_WIDTH), F32),
        ],
        2 * piece * width * (width + 4 * length),
        back_own,
        *back_got,
        mid,
        grad_rows,
        gain_feed,
        attn,
        query,
        probs,
        cosine,
        sine,
        *qo_near,
        *qo_far,
        *packets,
    )
    kv_got = [push(kv_sent[k - 1], -k) for k in others]

    down_own, down_got = plane_sum(down_near, down_far, chips)
    (block_output,) = call(
        down_end_kernel, [array((width, piece), F32)], [], 1e6, mid, down_own, *down_got
    )

    feed_got = [cross(feed_grads[k], k) for k in others]
    (feed_own,) = call(
        feed_end_kernel, [array((size, 3 * units, cut), BF)], [], 1e6, feed_grads[0], *feed_got
    )
    feed_back = lax.all_to_all(feed_own, "batch", split_axis=0, concat_axis=0, tiled=True)
    gate_done, up_done, down_done = call(
        feed_done_kernel,
        [
            array(gate_weight.shape, F32),
            array(up_weight.shape, F32),
            array(down_weight.shape[::-1], F32),
        ],
        [],
        1e6,
        feed_back.reshape(size, 3, units, cut),
    )

    shape = (line, 2, cut, qo_cols)
    *qo_grads, base = call(
        functools.partial(query_grad_kernel, chips),
        [array(shape, BF)] * size + [array((size, piece, cut), F32)],
        [((size, piece, cut), BF)] * 2 + [((line, piece, qo_cols), BF)] * 2,
        6 * piece * width * width,
        hidden_attn,
        grad_query,
        attn,
        grad_mid_low,
        *qo_near,
        *qo_far,
    )
    qo_own, qo_got = plane_sum(qo_grads[:chips], qo_grads[chips:], chips)
    block = (2, cut, qo_cols)
    qo_own, *qo_sent = call(
        functools.partial(qo_line_kernel, chips),
        [array(block, F32)] + [array(block, BF)] * (line - 1),
        [],
        1e6,
        qo_own,
        *qo_got,
    )
    qo_got = [cross(qo_sent[k - 1], k) for k in others]
    query_done, output_done = call(
        qo_end_kernel, [array((cut, qo_cols), F32)] * 2, [], 1e6, qo_own, *qo_got
    )

    each = width // kv_cols
    extra = -(-2 * each // 16) * 16
    shape = (line * cut + extra, kv_cols)
    input_grad, *kv_grads = call(
        functools.partial(input_grad_kernel, chips, line),
        [array((width, piece), F32)] + [array(shape, BF)] * size,
        [
            ((size, piece, cut), BF),
            ((piece, 2 * KV_WIDTH), BF),
            ((line, piece, kv_cols), BF),
            ((size, piece, cut), F32),
        ],
        4 * piece * width * 2 * KV_WIDTH,
        kv_own,
        *kv_got,
        rows,
        gain_attn,
        hidden_attn,
        grad_mid,
        base,
        cosine,
        sine,
        feed_term,
        *kv_near,
        *kv_far,
    )
    kv_own, kv_got = plane_sum(kv_grads[:chips], kv_grads[chips:], chips)
    kv_own, own_gains, *kv_sent = call(
        functools.partial(kv_line_kernel, chips, line),
        [array((cut, kv_cols), F32), array((extra, kv_cols), F32)]
        + [array((cut + extra, kv_cols), BF)] * (line - 1),
        [],
        1e6,
        kv_own,
        *kv_got,
    )
    kv_got = [cross(kv_sent[k - 1], k) for k in others]
    key_done, value_done, attn_gain_sum, feed_gain_sum = call(
        functools.partial(kv_end_kernel, line),
        [array((kv_cols // 2, cut), F32)] * 2 + [array((1, width), F32)] * 2,
        [],
        1e6,
        kv_own,
        own_gains,
        *kv_got,
    )
    return (
        block_output.T[None],
        input_grad.T[None],
        attn_gain_sum[0],
        query_done,
        key_done.T,
        value_done.T,
        output_done,
        feed_gain_sum[0],
        gate_done,
        up_done,
        down_done.T,
    )


def solution(mesh):
    both = P("batch", "seq")
    tokens = P("batch", "seq", None)
    in_specs = (tokens, both, P(), both, both, both, both, P(), both, both, P("seq", "batch"), tokens)
    out_specs = (tokens, tokens, P(), both, both, both, both, P(), both, both, P("seq", "batch"))

    return jax.shard_map(shards, mesh=mesh, in_specs=in_specs, out_specs=out_specs, check_vma=False)
```

```python
import functools
import math

import jax
import jax.numpy as jnp
from jax import lax
from jax.experimental import pallas as pl
from jax.experimental.pallas import tpu as pltpu
from jax.sharding import PartitionSpec as P


HEADS = 15
KV_HEADS = 5
HEAD_DIM = 64
GROUPS = HEADS // KV_HEADS
KV_WIDTH = KV_HEADS * HEAD_DIM
HALF = HEAD_DIM // 2
INV_ROOT = 1.0 / HEAD_DIM**0.5
BF = jnp.bfloat16
F32 = jnp.float32
ROOM = 6


def rotary_tables(positions):
    expon = jnp.arange(HALF, dtype=F32) * (2.0 / HEAD_DIM)
    inverse = jnp.power(F32(10000.0), -expon)
    angles = positions[:, None] * inverse[None, :]
    return jnp.cos(angles), jnp.sin(angles)


def mmul(left, right):
    return jnp.dot(left, right, preferred_element_type=F32)


def left_mmul(left, right):
    return lax.dot_general(left, right, (((0,), (0,)), ((), ())), preferred_element_type=F32)


def right_mmul(left, right):
    return lax.dot_general(left, right, (((1,), (1,)), ((), ())), preferred_element_type=F32)


def head_of(h):
    return slice(h * HEAD_DIM, (h + 1) * HEAD_DIM)


def tables(cosine, sine):
    c, d = cosine[...], sine[...]
    return jnp.concatenate([c, c], 1), jnp.concatenate([-d, d], 1)


def swapped(x):
    return jnp.concatenate([x[:, HALF:], x[:, :HALF]], 1)


def rms_scale(rows):
    return lax.rsqrt(jnp.mean(rows * rows, -1, keepdims=True) + 1e-05)


def norm_back(grad_out, normed, scale, gain):
    scaled = grad_out * gain
    inner = jnp.mean(scaled * normed, -1, keepdims=True)
    return (scale * (scaled - normed * inner), jnp.sum(grad_out * normed, 0, keepdims=True))


def split_lanes(ref, value, count):
    wide = value.shape[1] // count
    for j in range(count):
        ref[j] = value[:, j * wide : (j + 1) * wide]


def join_lanes(ref, count):
    return jnp.concatenate([ref[j] for j in range(count)], 1)


def blocks(near, far):
    b = lax.axis_index("batch")
    out = []
    for core, refs in ((0, near), (1, far)):
        for m, ref in enumerate(refs):
            out.append((ref, core, m, b ^ (2 * m + core)))
    return out


def take(refs, *counts):
    out = []
    at = 0
    for n in counts:
        out.append(refs[at] if n is None else refs[at : at + n])
        at += 1 if n is None else n
    assert at == len(refs)
    return out


def kv_kernel(chips, *refs):
    rows, gain, cosine, sine, seg, near, far, hidden, packet, hid3, acc4 = take(
        refs, *[None] * 5, chips, chips, *[None] * 4
    )
    line = near[0].shape[0]
    s = lax.axis_index("seq")
    piece = rows.shape[1]
    cos, sin = tables(cosine, sine)
    x = rows[...].T
    hid = (x * rms_scale(x) * gain[...]).astype(BF)
    hidden[...] = hid
    split_lanes(hid3, hid, hid3.shape[0])

    def body(k, carry):
        acc = 0.0
        for ref, _, m, at in blocks(near, far):
            acc = acc + mmul(hid3[at], ref[k])
        acc4[s ^ k] = acc
        return carry

    lax.fori_loop(0, line, body, 0)
    wide = near[0].shape[-1] // 2
    keys = jnp.concatenate([acc4[p, :, :wide] for p in range(line)], 1)
    values = jnp.concatenate([acc4[p, :, wide:] for p in range(line)], 1)
    for h in range(KV_HEADS):
        u = keys[:, head_of(h)]
        packet[:piece, head_of(h)] = (u * cos + swapped(u) * sin).astype(BF)
    packet[:piece, KV_WIDTH:] = values.astype(BF)
    packet[piece:, :] = jnp.zeros((packet.shape[0] - piece, packet.shape[1]), BF)
    packet[piece:, :piece] = jnp.broadcast_to(
        seg[...].astype(F32), (packet.shape[0] - piece, piece)
    ).astype(BF)


def query_kernel(chips, *refs):
    hidden, cosine, sine, near, far, query, hid3, acc4 = take(
        refs, None, None, None, chips, chips, None, None, None
    )
    line = near[0].shape[0]
    s = lax.axis_index("seq")
    cos, sin = tables(cosine, sine)
    split_lanes(hid3, hidden[...], hid3.shape[0])

    def body(k, carry):
        acc = 0.0
        for ref, _, m, at in blocks(near, far):
            acc = acc + mmul(hid3[at], ref[k, 0])
        acc4[s ^ k] = acc
        return carry

    lax.fori_loop(0, line, body, 0)
    full = join_lanes(acc4, line)
    for h in range(HEADS):
        u = full[:, head_of(h)]
        query[:, head_of(h)] = (u * cos + swapped(u) * sin).astype(BF)


def group_rows(ref, g):
    return jnp.concatenate([ref[:, head_of(GROUPS * g + i)] for i in range(GROUPS)], 0)


def slot_rows(packets, piece, lanes):
    return jnp.concatenate([p[:piece, lanes] for p in packets], 0)


def attention_kernel(chips, line, *refs):
    query, packets, rows, seg, gain, near, far, *rest = take(
        refs, None, line, None, None, None, chips, chips, *[None] * 7
    )
    probs, attn, mid, hidden, bias, att3, acc4 = rest
    s = lax.axis_index("seq")
    piece = rows.shape[1]
    mine = jnp.broadcast_to(seg[...].astype(F32), (piece, piece)).T
    at = lax.broadcasted_iota(jnp.int32, (piece, piece), 0)
    key = lax.broadcasted_iota(jnp.int32, (piece, piece), 1)
    for k in range(line):
        same = mine == packets[k][piece : piece + 1, :piece].astype(F32)
        ok = same & (key - k * piece <= at) & (key + (s - k) * piece >= 0)
        bias[:, k * piece : (k + 1) * piece] = jnp.where(ok, 0.0, -jnp.inf)
    for g in range(KV_HEADS):
        keys = slot_rows(packets, piece, head_of(g))
        values = slot_rows(packets, piece, head_of(KV_HEADS + g))
        scores = right_mmul(group_rows(query, g), keys) * INV_ROOT
        scores = scores + jnp.concatenate([bias[...]] * GROUPS, 0)
        raised = jnp.exp(scores - jnp.max(scores, -1, keepdims=True))
        weights = raised / jnp.sum(raised, -1, keepdims=True)
        probs[g] = weights
        out = mmul(weights.astype(BF), values).astype(BF)
        for i in range(GROUPS):
            attn[:, head_of(GROUPS * g + i)] = out[i * piece : (i + 1) * piece]
    split_lanes(att3, attn[...], att3.shape[0])

    def body(k, carry):
        acc = 0.0
        for ref, _, m, j in blocks(near, far):
            acc = acc + mmul(att3[j], ref[k, 1])
        acc4[s ^ k] = acc
        return carry

    lax.fori_loop(0, line, body, 0)
    x = rows[...].T + join_lanes(acc4, line)
    mid[...] = x
    hidden[...] = (x * rms_scale(x) * gain[...]).astype(BF)


def load_all(refs, scratch, sems):
    rows = refs[0].shape[0]
    copies = [
        pltpu.make_async_copy(ref, scratch.at[pl.ds(i * rows, rows)], sems.at[i])
        for i, ref in enumerate(refs)
    ]
    for copy in copies:
        copy.start()
    return copies


def load_slots(own, right, left, slots):
    s = lax.axis_index("seq")
    line = slots.shape[0]
    pltpu.sync_copy(own, slots.at[s])
    for far in range(1, line):

        @pl.when(s >= far)
        def _():
            pltpu.sync_copy(right[far - 1], slots.at[s - far])

        @pl.when(s + far < line)
        def _():
            pltpu.sync_copy(left[far - 1], slots.at[s + far])


def feed_kernel(chips, line, tile, *refs):
    hid, low, own, right, left, back_near, back_far, gate_s, up_s, inner_s, *scratch = take(
        refs, 2 * chips, 2 * chips, None, line - 1, line - 1, None, chips, *[None] * 12
    )
    slots, gate_w, up_w, down_w, hid_s, low_s, far_s, sems, far_sems = scratch
    copies = load_all(hid, hid_s, sems) + load_all(low, low_s, sems.at[pl.ds(2 * chips, 2 * chips)])
    load_slots(own, right, left, slots)
    piece = hid[0].shape[0]
    units = own.shape[0] // 3
    for k in range(line):
        span = slice(k * units, (k + 1) * units)
        gate_w[span] = slots[k, :units]
        up_w[span] = slots[k, units : 2 * units]
        down_w[span] = slots[k, 2 * units :]
    for copy in copies:
        copy.wait()
    half = chips * piece

    def run(back, base):
        def body(i, carry):
            span = pl.ds(pl.multiple_of(i * tile, tile), tile)
            read = pl.ds(pl.multiple_of(base + i * tile, tile), tile)
            h = hid_s[read]
            gate = right_mmul(h, gate_w[...])
            up = right_mmul(h, up_w[...])
            inner_grad = right_mmul(low_s[read], down_w[...])
            sigma = jax.nn.sigmoid(gate)
            inner_s[read] = (gate * sigma * up).astype(BF)
            grad_up = (inner_grad * gate * sigma).astype(BF)
            grad_gate = (inner_grad * up * sigma * (1.0 + gate * (1.0 - sigma))).astype(BF)
            gate_s[read] = grad_gate
            up_s[read] = grad_up
            total_back = mmul(grad_gate, gate_w[...]) + mmul(grad_up, up_w[...])
            back[span] = total_back.astype(BF)
            return carry

        lax.fori_loop(0, half // tile, body, 0)

    run(far_s, half)
    sends = [
        pltpu.make_async_copy(far_s.at[pl.ds(m * piece, piece)], back_far[m], far_sems.at[m])
        for m in range(chips)
    ]
    for send in sends:
        send.start()
    run(back_near, 0)
    for send in sends:
        send.wait()


def feed_grad_kernel(chips, line, *refs):
    hid, low, own, right, left, gate_s, up_s, inner_s, down_near, down_far, *rest = take(
        refs,
        *(2 * chips, 2 * chips, None, line - 1, line - 1, None, None, None, None, chips),
        *(None, line - 1, line - 1, *[None] * 6),
    )
    mine, to_left, to_right, slots, down_w, hid_s, low_s, terms, sems = rest
    s = lax.axis_index("seq")
    copies = load_all(hid, hid_s, sems) + load_all(low, low_s, sems.at[pl.ds(2 * chips, 2 * chips)])
    load_slots(own, right, left, slots)
    piece = hid[0].shape[0]
    units = own.shape[0] // 3
    for k in range(line):
        down_w[k * units : (k + 1) * units] = slots[k, 2 * units :]
    for copy in copies:
        copy.wait()
    half = chips * piece
    for m in range(chips):
        span = slice(m * piece, (m + 1) * piece)
        far = slice(half + m * piece, half + (m + 1) * piece)
        down_near[span] = mmul(inner_s[span], down_w[...]).astype(BF)
        down_far[m][...] = mmul(inner_s[far], down_w[...]).astype(BF)
    for n, (a, b) in enumerate(((gate_s, hid_s), (up_s, hid_s), (inner_s, low_s))):
        term = left_mmul(a[...], b[...])
        for k in range(line):
            terms[k, n * units : (n + 1) * units] = term[k * units : (k + 1) * units]
    mine[...] = terms[s]
    for k in range(1, line):
        for out, ok, at in (
            (to_left[k - 1], s >= k, s - k),
            (to_right[k - 1], s + k < line, s + k),
        ):

            @pl.when(ok)
            def _():
                out[...] = terms[at].astype(BF)

            @pl.when(jnp.logical_not(ok))
            def _():
                out[...] = jnp.zeros(out.shape, BF)


def add_kernel(*refs):
    count = len(refs) // 3
    for i in range(count):
        a, b, out = refs[2 * i], refs[2 * i + 1], refs[2 * count + i]
        out[...] = (a[...].astype(F32) + b[...].astype(F32)).astype(BF)


def middle_kernel(chips, line, *refs):
    parts, mid, out_grad, gain, attn, query, probs, cosine, sine, near, far, packets, *rest = take(
        refs, chips, *[None] * 8, chips, chips, line, *[None] * 4, line, *[None] * 4
    )
    grad_mid, gain_term, grad_low, grad_query, slots, low4, att3, grad_attn, grad_kv = rest
    s = lax.axis_index("seq")
    piece = mid.shape[0]
    cos, sin = tables(cosine, sine)
    grad = parts[0][...].astype(F32)
    for part in parts[1:]:
        grad = grad + part[...].astype(F32)
    x = mid[...]
    scale = rms_scale(x)
    back, term = norm_back(grad, x * scale, scale, gain[...])
    gain_term[...] = term
    whole = out_grad[...].T + back
    grad_mid[...] = whole
    low = whole.astype(BF)
    grad_low[...] = low
    split_lanes(low4, low, line)
    for ref, _, m, j in blocks(near, far):
        acc = 0.0
        for k in range(line):
            acc = acc + right_mmul(low4[s ^ k], ref[k, 1])
        att3[j] = acc.astype(BF)
    grad_attn[...] = join_lanes(att3, att3.shape[0])
    for g in range(KV_HEADS):
        keys = slot_rows(packets, piece, head_of(g))
        values = slot_rows(packets, piece, head_of(KV_HEADS + g))
        q = group_rows(query, g)
        ga = group_rows(grad_attn, g)
        at = group_rows(attn, g)
        dots = jnp.sum(ga.astype(F32) * at.astype(F32), -1, keepdims=True)
        weights = probs[g]
        gs = (weights * (right_mmul(ga, values) - dots) * INV_ROOT).astype(BF)
        gq = mmul(gs, keys)
        for i in range(GROUPS):
            u = gq[i * piece : (i + 1) * piece]
            h = GROUPS * g + i
            grad_query[:, head_of(h)] = (u * cos - swapped(u) * sin).astype(BF)
        grad_kv[:, head_of(g)] = left_mmul(gs, q)
        grad_kv[:, head_of(KV_HEADS + g)] = left_mmul(weights.astype(BF), ga)
    for k in range(line):
        slots[k][...] = grad_kv[k * piece : (k + 1) * piece].astype(slots[k].dtype)


def query_grad_kernel(chips, *refs):
    hidden, grad_query, attn, grad_low, near, far, out_near, out_far, back, *scratch = take(
        refs, *[None] * 4, chips, chips, chips, chips, *[None] * 5
    )
    hid3, att3, gq4, low4 = scratch
    line = near[0].shape[0]
    s = lax.axis_index("seq")
    size = hid3.shape[0]
    split_lanes(hid3, hidden[...], size)
    split_lanes(att3, attn[...], size)
    split_lanes(gq4, grad_query[...], line)
    split_lanes(low4, grad_low[...], line)

    def body(k, carry):
        for ref, core, m, j in blocks(near, far):
            out = (out_near, out_far)[core][m]
            out[k, 0] = left_mmul(hid3[j], gq4[s ^ k]).astype(BF)
            out[k, 1] = left_mmul(att3[j], low4[s ^ k]).astype(BF)
        return carry

    lax.fori_loop(0, line, body, 0)
    for ref, _, m, j in blocks(near, far):
        acc = 0.0
        for k in range(line):
            acc = acc + right_mmul(gq4[s ^ k], ref[k, 0])
        back[j] = acc


def input_grad_kernel(chips, line, *refs):
    parts, rows, gain, hidden, grad_mid, base, cosine, sine, feed_term, near, far, *rest = take(
        refs, line, *[None] * 8, chips, chips, None, 2 * chips, *[None] * 4
    )
    result, outs, hid3, full, gkv4, x3 = take(rest, *[None] * 6)
    cos, sin = tables(cosine, sine)
    s = lax.axis_index("seq")
    size = hid3.shape[0]
    both = parts[0][...]
    for part in parts[1:]:
        both = both + part[...].astype(F32)
    for h in range(KV_HEADS):
        u = both[:, head_of(h)]
        full[:, head_of(h)] = (u * cos - swapped(u) * sin).astype(BF)
    full[:, KV_WIDTH:] = both[:, KV_WIDTH:].astype(BF)
    wide = KV_WIDTH // line
    for p in range(line):
        gkv4[p, :, :wide] = full[:, p * wide : (p + 1) * wide]
        gkv4[p, :, wide:] = full[:, KV_WIDTH + p * wide : KV_WIDTH + (p + 1) * wide]
    split_lanes(hid3, hidden[...], size)
    for ref, _, m, j in blocks(near, far):
        acc = base[j]
        for k in range(line):
            acc = acc + right_mmul(gkv4[s ^ k], ref[k])
        x3[j] = acc
    x = rows[...].T
    scale = rms_scale(x)
    back, term = norm_back(join_lanes(x3, size), x * scale, scale, gain[...])
    result[...] = (grad_mid[...] + back).T
    rows_of = hid3.shape[2]
    lanes = 2 * wide
    each = x.shape[1] // lanes
    for ref, core, m, j in blocks(near, far):
        out = outs[core * chips + m]
        for k in range(line):
            span = slice(k * rows_of, (k + 1) * rows_of)
            out[span] = left_mmul(hid3[j], gkv4[s ^ k]).astype(BF)
        base_row = line * rows_of
        out[base_row:] = jnp.zeros((out.shape[0] - base_row, lanes), BF)
        for n, value in enumerate((term, feed_term[...])):
            for i in range(each):
                at = base_row + n * each + i
                out[at : at + 1] = value[:, i * lanes : (i + 1) * lanes].astype(BF)


def join_kernel(key, value, query, output, out):
    a = key.shape[0]
    b = query.shape[1]
    out[:, :a] = key[...].T
    out[:, a : 2 * a] = value[...].T
    out[:, 2 * a : 2 * a + b] = query[...]
    out[:, 2 * a + b :] = output[...]


def stack_kernel(line, *refs):
    slots, kv, qo = take(refs, line, None, None)
    a = kv.shape[2]
    b = qo.shape[3]
    for k in range(line):
        kv[k] = slots[k][:, :a]
        qo[k, 0] = slots[k][:, a : a + b]
        qo[k, 1] = slots[k][:, a + b :]


def cast_kernel(grad, out):
    out[...] = grad[...].T.astype(BF)


def spread_kernel(gate, up, down, out):
    units = out.shape[2]
    for j in range(out.shape[0]):
        span = slice(j * units, (j + 1) * units)
        out[j, 0] = gate[:, span].T
        out[j, 1] = up[:, span].T
        out[j, 2] = down[:, span].T


def arrange_kernel(got, out):
    cut = got.shape[3]
    units = got.shape[2]
    for j in range(got.shape[0]):
        for n in range(3):
            out[n * units : (n + 1) * units, j * cut : (j + 1) * cut] = got[j, n]


def pair_sum_kernel(chips, *refs):
    near, got, own, outs = take(refs, chips, chips, None, chips - 1)
    own[...] = near[0][...].astype(F32) + got[0][...].astype(F32)
    for m in range(1, chips):
        outs[m - 1][...] = (near[m][...].astype(F32) + got[m][...].astype(F32)).astype(BF)


def stack_sum_kernel(chips, near, *refs):
    got, own, outs = take(refs, chips, None, chips - 1)
    rows = own.shape[0]
    own[...] = near[:rows].astype(F32) + got[0][...].astype(F32)
    for m in range(1, chips):
        mine = near[m * rows : (m + 1) * rows].astype(F32)
        outs[m - 1][...] = (mine + got[m][...].astype(F32)).astype(BF)


def down_end_kernel(mid, own, *refs):
    *got, out = refs
    out[...] = (mid[...] + tree([own[...]] + [g[...].astype(F32) for g in got])).T


def feed_end_kernel(own, *refs):
    left, right, out = refs
    whole = own[...] + left[...].astype(F32) + right[...].astype(F32)
    split_lanes(out, whole.astype(BF), out.shape[0])


def feed_done_kernel(got, gate, up, down):
    units = got.shape[2]
    for j in range(got.shape[0]):
        span = slice(j * units, (j + 1) * units)
        gate[:, span] = got[j, 0].astype(F32).T
        up[:, span] = got[j, 1].astype(F32).T
        down[:, span] = got[j, 2].astype(F32).T


def qo_line_kernel(chips, own, *refs):
    got, mine, sent = take(refs, chips - 1, None, len(refs) - chips)
    for k in range(own.shape[0]):
        whole = tree([own[k]] + [g[k].astype(F32) for g in got])
        if k == 0:
            mine[...] = whole
        else:
            sent[k - 1][...] = whole.astype(BF)


def qo_end_kernel(own, *refs):
    *got, query, output = refs
    query[...] = tree([own[0]] + [g[0].astype(F32) for g in got])
    output[...] = tree([own[1]] + [g[1].astype(F32) for g in got])


def kv_line_kernel(chips, line, own, *refs):
    got, mine, gains, sent = take(refs, chips - 1, None, None, line - 1)
    cut = mine.shape[0]
    last = slice(line * cut, None)
    term = tree([own[last].astype(BF).astype(F32)] + [g[last].astype(F32) for g in got]).astype(BF)
    gains[...] = term.astype(F32)
    for k in range(line):
        span = slice(k * cut, (k + 1) * cut)
        whole = tree([own[span]] + [g[span].astype(F32) for g in got])
        if k == 0:
            mine[...] = whole
        else:
            sent[k - 1][:cut] = whole.astype(BF)
            sent[k - 1][cut:] = term


def kv_end_kernel(line, own, own_gains, *refs):
    got, keys, values, attn_gain, feed_gain = take(refs, line - 1, *[None] * 4)
    cut, lanes = own.shape
    whole = tree([own[...]] + [g[:cut].astype(F32) for g in got])
    keys[...] = whole[:, : lanes // 2].T
    values[...] = whole[:, lanes // 2 :].T
    gains = tree([own_gains[...]] + [g[cut:].astype(F32) for g in got])
    each = attn_gain.shape[1] // lanes
    for n, out in enumerate((attn_gain, feed_gain)):
        for i in range(each):
            out[:, i * lanes : (i + 1) * lanes] = gains[n * each + i : n * each + i + 1]


def padded(a):
    if len(a.shape) < 2:
        return 4096
    size = jnp.dtype(a.dtype).itemsize
    *outer, rows, lanes = a.shape
    tile = 32 // size
    return math.prod(outer) * (-(-rows // tile) * tile) * (-(-lanes // 128) * 128) * size


def call(kernel, outs, scratch, flops, *args, far=0, far_outs=(), grant=True):
    sizes = [a.size * a.dtype.itemsize for a in (*args, *outs)]
    vmem = pl.BlockSpec(memory_space=pltpu.VMEM)
    free = pl.BlockSpec(memory_space=pl.ANY)
    held = [a for i, a in enumerate(args) if i >= far]
    held += [a for i, a in enumerate(outs) if i not in far_outs]
    held += [array(*x) for x in scratch if isinstance(x, tuple)]
    limit = min(sum(padded(a) for a in held) + ROOM * 2**20, 60 * 1024 * 2**10) if grant else None
    return pl.pallas_call(
        kernel,
        out_shape=outs,
        in_specs=[free if i < far else vmem for i in range(len(args))],
        out_specs=[free if i in far_outs else vmem for i in range(len(outs))],
        scratch_shapes=[x if not isinstance(x, tuple) else pltpu.VMEM(x[0], x[1]) for x in scratch],
        cost_estimate=pl.CostEstimate(
            flops=int(flops), bytes_accessed=sum(sizes), transcendentals=0
        ),
        compiler_params=pltpu.CompilerParams(vmem_limit_bytes=limit),
    )(*args)


def array(shape, dtype):
    return jax.ShapeDtypeStruct(shape, dtype)


def flip(x, bits):
    n = lax.axis_size("batch")
    return lax.ppermute(x, "batch", [(i, i ^ bits) for i in range(n)])


def cross(x, bits):
    n = lax.axis_size("seq")
    return lax.ppermute(x, "seq", [(i, i ^ bits) for i in range(n)])


def push(x, by):
    n = lax.axis_size("seq")
    pairs = [(i, i + by) for i in range(n) if 0 <= i + by < n]
    return lax.ppermute(x, "seq", pairs)


def tree(terms):
    while len(terms) > 1:
        terms = [terms[i] + terms[i + 1] for i in range(0, len(terms), 2)]
    return terms[0]


def plane_hops(x, chips):
    return [x] + [flip(x, 2 * m) for m in range(1, chips)]


def pair_swap(xs):
    return [flip(x, 1) for x in xs]


def plane_sum(near, far, chips):
    got = pair_swap(far)
    block = far[0].shape
    one = not isinstance(near, (list, tuple))
    own, *low = call(
        functools.partial(stack_sum_kernel if one else pair_sum_kernel, chips),
        [array(block, F32)] + [array(block, BF)] * (chips - 1),
        [],
        1e6,
        *([near] if one else near),
        *got,
    )
    return own, [flip(low[m - 1], 2 * m) for m in range(1, chips)]


def line_chain(x, line):
    out = []
    for by in (1, -1):
        held = x
        got = []
        for k in range(1, line):
            held = step(held, by, k)
            got.append(held)
        out.append(got)
    return out


def hand(x, by, k):
    n = lax.axis_size("seq")
    senders = range(n - k) if by > 0 else range(k, n)
    return lax.ppermute(x, "seq", [(i, i + by) for i in senders])


def step(x, by, k):
    n = lax.axis_size("seq")
    senders = range(k - 1, n - 1) if by > 0 else range(1, n - k + 1)
    return lax.ppermute(x, "seq", [(i, i + by) for i in senders])


def shards(
    activations,
    segment_ids,
    attention_gain,
    query_weight,
    key_weight,
    value_weight,
    output_weight,
    feed_gain,
    gate_weight,
    up_weight,
    down_weight,
    out_grad,
):
    piece, width = activations.shape[1:]
    line = lax.axis_size("seq")
    size = lax.axis_size("batch")
    length = piece * line
    chips = size // 2
    cut = width // size
    rows = activations[0].T
    grad_rows = out_grad[0].T
    s = lax.axis_index("seq")
    positions = s * piece + jnp.arange(piece, dtype=jnp.int32)
    cosine, sine = rotary_tables(positions.astype(F32))
    gain_attn = attention_gain[None]
    gain_feed = feed_gain[None]
    units = gate_weight.shape[1] // size
    others = range(1, line)

    kv_cols = 2 * key_weight.shape[1]
    qo_cols = query_weight.shape[1]
    (own,) = call(
        join_kernel,
        [array((cut, kv_cols + 2 * qo_cols), BF)],
        [],
        1e5,
        key_weight.T,
        value_weight.T,
        query_weight,
        output_weight,
        grant=False,
    )
    kv_slots, qo_slots = call(
        functools.partial(stack_kernel, line),
        [array((line, cut, kv_cols), BF), array((line, 2, cut, qo_cols), BF)],
        [],
        1e5,
        own,
        *[cross(own, k) for k in others],
    )
    kv_near = plane_hops(kv_slots, chips)
    kv_far = pair_swap(kv_near)
    qo_near = plane_hops(qo_slots, chips)
    qo_far = pair_swap(qo_near)

    (local,) = call(
        spread_kernel,
        [array((size, 3, units, cut), BF)],
        [],
        1e5,
        gate_weight,
        up_weight,
        down_weight.T,
        grant=False,
    )
    spread = lax.all_to_all(local, "batch", split_axis=0, concat_axis=0, tiled=True)
    (feed_own,) = call(arrange_kernel, [array((3 * units, width), BF)], [], 1e5, spread)
    feed_right, feed_left = line_chain(feed_own, line)

    (low,) = call(cast_kernel, [array((piece, width), BF)], [], 1e5, grad_rows, grant=False)
    low_near = plane_hops(low, chips)
    low_far = pair_swap(low_near)

    hidden_attn, packet = call(
        functools.partial(kv_kernel, chips),
        [array((piece, width), BF), array((piece + 8, 2 * KV_WIDTH), BF)],
        [((size, piece, cut), BF), ((line, piece, kv_cols), F32)],
        2 * piece * width * 2 * KV_WIDTH,
        rows,
        gain_attn,
        cosine,
        sine,
        segment_ids,
        *kv_near,
        *kv_far,
    )
    packets = [packet] + [push(packet, k) for k in others]
    (query,) = call(
        functools.partial(query_kernel, chips),
        [array((piece, width), BF)],
        [((size, piece, cut), BF), ((line, piece, qo_cols), F32)],
        2 * piece * width * width,
        hidden_attn,
        cosine,
        sine,
        *qo_near,
        *qo_far,
    )
    probs, attn, mid, hidden_feed = call(
        functools.partial(attention_kernel, chips, line),
        [
            array((KV_HEADS, GROUPS * piece, length), F32),
            array((piece, width), BF),
            array((piece, width), F32),
            array((piece, width), BF),
        ],
        [((piece, length), F32), ((size, piece, cut), BF), ((line, piece, qo_cols), F32)],
        2 * piece * width * (width + 2 * length),
        query,
        *packets,
        rows,
        segment_ids,
        gain_feed,
        *qo_near,
        *qo_far,
    )
    hid_near = plane_hops(hidden_feed, chips)
    hid_far = pair_swap(hid_near)
    flat = (chips * piece, width)
    tokens = size * piece
    act = (tokens, line * units)
    feed_in = [*hid_near, *hid_far, *low_near, *low_far, feed_own, *feed_right, *feed_left]
    slots = [((line, 3 * units, width), BF), ((line * units, width), BF)]
    both = [((tokens, width), BF)] * 2
    sems = pltpu.SemaphoreType.DMA((4 * chips,))
    back_near, *rest = call(
        functools.partial(feed_kernel, chips, line, 2 * piece),
        [array(flat, BF)] + [array((piece, width), BF)] * chips + [array(act, BF)] * 3,
        [
            slots[0],
            slots[1],
            slots[1],
            slots[1],
            *both,
            (flat, BF),
            sems,
            pltpu.SemaphoreType.DMA((chips,)),
        ],
        10 * tokens * width * line * units,
        *feed_in,
        far=len(feed_in),
        far_outs=range(1, chips + 1),
    )
    back_far, acts = rest[:chips], rest[chips:]
    back_own, back_got = plane_sum(back_near, back_far, chips)
    down_near, *rest = call(
        functools.partial(feed_grad_kernel, chips, line),
        [array(flat, BF)]
        + [array((piece, width), BF)] * chips
        + [array((3 * units, width), F32)]
        + [array((3 * units, width), BF)] * (2 * line - 2),
        [*slots, *both, ((line, 3 * units, width), F32), sems],
        8 * tokens * width * line * units,
        *feed_in,
        *acts,
        far=len(feed_in),
    )
    down_far, feed_grads = rest[:chips], rest[chips:]
    grad_mid, feed_term, grad_mid_low, grad_query, kv_own, *kv_sent = call(
        functools.partial(middle_kernel, chips, line),
        [
            array((piece, width), F32),
            array((1, width), F32),
            array((piece, width), BF),
            array((piece, width), BF),
            array((piece, 2 * KV_WIDTH), F32),
        ]
        + [array((piece, 2 * KV_WIDTH), BF)] * (line - 1),
        [
            ((line, piece, qo_cols), BF),
            ((size, piece, cut), BF),
            ((piece, width), BF),
            ((length, 2 * KV_WIDTH), F32),
        ],
        2 * piece * width * (width + 4 * length),
        back_own,
        *back_got,
        mid,
        grad_rows,
        gain_feed,
        attn,
        query,
        probs,
        cosine,
        sine,
        *qo_near,
        *qo_far,
        *packets,
    )
    kv_got = [push(kv_sent[k - 1], -k) for k in others]

    down_own, down_got = plane_sum(down_near, down_far, chips)
    (block_output,) = call(
        down_end_kernel, [array((width, piece), F32)], [], 1e6, mid, down_own, *down_got
    )

    to_left, to_right = feed_grads[1:line], feed_grads[line:]
    left, right = to_left[-1], to_right[-1]
    for k in range(line - 1, 0, -1):
        left = hand(left, -1, k)
        right = hand(right, 1, k)
        if k > 1:
            left, right = call(
                add_kernel,
                [array(left.shape, BF)] * 2,
                [],
                1e6,
                left,
                to_left[k - 2],
                right,
                to_right[k - 2],
            )
    (feed_own,) = call(
        feed_end_kernel, [array((size, 3 * units, cut), BF)], [], 1e6, feed_grads[0], left, right
    )
    feed_back = lax.all_to_all(feed_own, "batch", split_axis=0, concat_axis=0, tiled=True)
    gate_done, up_done, down_done = call(
        feed_done_kernel,
        [
            array(gate_weight.shape, F32),
            array(up_weight.shape, F32),
            array(down_weight.shape[::-1], F32),
        ],
        [],
        1e6,
        feed_back.reshape(size, 3, units, cut),
    )

    shape = (line, 2, cut, qo_cols)
    *qo_grads, base = call(
        functools.partial(query_grad_kernel, chips),
        [array(shape, BF)] * size + [array((size, piece, cut), F32)],
        [((size, piece, cut), BF)] * 2 + [((line, piece, qo_cols), BF)] * 2,
        6 * piece * width * width,
        hidden_attn,
        grad_query,
        attn,
        grad_mid_low,
        *qo_near,
        *qo_far,
    )
    qo_own, qo_got = plane_sum(qo_grads[:chips], qo_grads[chips:], chips)
    block = (2, cut, qo_cols)
    qo_own, *qo_sent = call(
        functools.partial(qo_line_kernel, chips),
        [array(block, F32)] + [array(block, BF)] * (line - 1),
        [],
        1e6,
        qo_own,
        *qo_got,
    )
    qo_got = [cross(qo_sent[k - 1], k) for k in others]
    query_done, output_done = call(
        qo_end_kernel, [array((cut, qo_cols), F32)] * 2, [], 1e6, qo_own, *qo_got
    )

    each = width // kv_cols
    extra = -(-2 * each // 16) * 16
    shape = (line * cut + extra, kv_cols)
    input_grad, *kv_grads = call(
        functools.partial(input_grad_kernel, chips, line),
        [array((width, piece), F32)] + [array(shape, BF)] * size,
        [
            ((size, piece, cut), BF),
            ((piece, 2 * KV_WIDTH), BF),
            ((line, piece, kv_cols), BF),
            ((size, piece, cut), F32),
        ],
        4 * piece * width * 2 * KV_WIDTH,
        kv_own,
        *kv_got,
        rows,
        gain_attn,
        hidden_attn,
        grad_mid,
        base,
        cosine,
        sine,
        feed_term,
        *kv_near,
        *kv_far,
    )
    kv_own, kv_got = plane_sum(kv_grads[:chips], kv_grads[chips:], chips)
    kv_own, own_gains, *kv_sent = call(
        functools.partial(kv_line_kernel, chips, line),
        [array((cut, kv_cols), F32), array((extra, kv_cols), F32)]
        + [array((cut + extra, kv_cols), BF)] * (line - 1),
        [],
        1e6,
        kv_own,
        *kv_got,
    )
    kv_got = [cross(kv_sent[k - 1], k) for k in others]
    key_done, value_done, attn_gain_sum, feed_gain_sum = call(
        functools.partial(kv_end_kernel, line),
        [array((kv_cols // 2, cut), F32)] * 2 + [array((1, width), F32)] * 2,
        [],
        1e6,
        kv_own,
        own_gains,
        *kv_got,
    )
    return (
        block_output.T[None],
        input_grad.T[None],
        attn_gain_sum[0],
        query_done,
        key_done.T,
        value_done.T,
        output_done,
        feed_gain_sum[0],
        gate_done,
        up_done,
        down_done.T,
    )


def solution(mesh):
    both = P("batch", "seq")
    tokens = P("batch", "seq", None)
    in_specs = (tokens, both, P(), both, both, both, both, P(), both, both, P("seq", "batch"), tokens)
    out_specs = (tokens, tokens, P(), both, both, both, both, P(), both, both, P("seq", "batch"))

    return jax.shard_map(shards, mesh=mesh, in_specs=in_specs, out_specs=out_specs, check_vma=False)
```

```python
import functools
import math

import jax
import jax.numpy as jnp
from jax import lax
from jax.experimental import pallas as pl
from jax.experimental.pallas import tpu as pltpu
from jax.sharding import PartitionSpec as P


HEADS = 15
KV_HEADS = 5
HEAD_DIM = 64
GROUPS = HEADS // KV_HEADS
KV_WIDTH = KV_HEADS * HEAD_DIM
HALF = HEAD_DIM // 2
INV_ROOT = 1.0 / HEAD_DIM**0.5
BF = jnp.bfloat16
F32 = jnp.float32
ROOM = 6


def rotary_tables(positions):
    expon = jnp.arange(HALF, dtype=F32) * (2.0 / HEAD_DIM)
    inverse = jnp.power(F32(10000.0), -expon)
    angles = positions[:, None] * inverse[None, :]
    return jnp.cos(angles), jnp.sin(angles)


def mmul(left, right):
    return jnp.dot(left, right, preferred_element_type=F32)


def left_mmul(left, right):
    return lax.dot_general(left, right, (((0,), (0,)), ((), ())), preferred_element_type=F32)


def right_mmul(left, right):
    return lax.dot_general(left, right, (((1,), (1,)), ((), ())), preferred_element_type=F32)


def head_of(h):
    return slice(h * HEAD_DIM, (h + 1) * HEAD_DIM)


def tables(cosine, sine):
    c, d = cosine[...], sine[...]
    return jnp.concatenate([c, c], 1), jnp.concatenate([-d, d], 1)


def swapped(x):
    return jnp.concatenate([x[:, HALF:], x[:, :HALF]], 1)


def rms_scale(rows):
    return lax.rsqrt(jnp.mean(rows * rows, -1, keepdims=True) + 1e-05)


def norm_back(grad_out, normed, scale, gain):
    scaled = grad_out * gain
    inner = jnp.mean(scaled * normed, -1, keepdims=True)
    return (scale * (scaled - normed * inner), jnp.sum(grad_out * normed, 0, keepdims=True))


def split_lanes(ref, value, count):
    wide = value.shape[1] // count
    for j in range(count):
        ref[j] = value[:, j * wide : (j + 1) * wide]


def join_lanes(ref, count):
    return jnp.concatenate([ref[j] for j in range(count)], 1)


def blocks(near, far):
    b = lax.axis_index("batch")
    out = []
    for core, refs in ((0, near), (1, far)):
        for m, ref in enumerate(refs):
            out.append((ref, core, m, b ^ (2 * m + core)))
    return out


def take(refs, *counts):
    out = []
    at = 0
    for n in counts:
        out.append(refs[at] if n is None else refs[at : at + n])
        at += 1 if n is None else n
    assert at == len(refs)
    return out


def kv_kernel(chips, *refs):
    rows, gain, cosine, sine, seg, near, far, hidden, packet, hid3, acc4 = take(
        refs, *[None] * 5, chips, chips, *[None] * 4
    )
    line = near[0].shape[0]
    s = lax.axis_index("seq")
    piece = rows.shape[1]
    cos, sin = tables(cosine, sine)
    x = rows[...].T
    hid = (x * rms_scale(x) * gain[...]).astype(BF)
    hidden[...] = hid
    split_lanes(hid3, hid, hid3.shape[0])

    def body(k, carry):
        acc = 0.0
        for ref, _, m, at in blocks(near, far):
            acc = acc + mmul(hid3[at], ref[k])
        acc4[s ^ k] = acc
        return carry

    lax.fori_loop(0, line, body, 0)
    wide = near[0].shape[-1] // 2
    keys = jnp.concatenate([acc4[p, :, :wide] for p in range(line)], 1)
    values = jnp.concatenate([acc4[p, :, wide:] for p in range(line)], 1)
    for h in range(KV_HEADS):
        u = keys[:, head_of(h)]
        packet[:piece, head_of(h)] = (u * cos + swapped(u) * sin).astype(BF)
    packet[:piece, KV_WIDTH:] = values.astype(BF)
    packet[piece:, :] = jnp.zeros((packet.shape[0] - piece, packet.shape[1]), BF)
    packet[piece:, :piece] = jnp.broadcast_to(
        seg[...].astype(F32), (packet.shape[0] - piece, piece)
    ).astype(BF)


def query_kernel(chips, *refs):
    hidden, cosine, sine, near, far, query, hid3, acc4 = take(
        refs, None, None, None, chips, chips, None, None, None
    )
    line = near[0].shape[0]
    s = lax.axis_index("seq")
    cos, sin = tables(cosine, sine)
    split_lanes(hid3, hidden[...], hid3.shape[0])

    def body(k, carry):
        acc = 0.0
        for ref, _, m, at in blocks(near, far):
            acc = acc + mmul(hid3[at], ref[k, 0])
        acc4[s ^ k] = acc
        return carry

    lax.fori_loop(0, line, body, 0)
    full = join_lanes(acc4, line)
    for h in range(HEADS):
        u = full[:, head_of(h)]
        query[:, head_of(h)] = (u * cos + swapped(u) * sin).astype(BF)


def group_rows(ref, g):
    return jnp.concatenate([ref[:, head_of(GROUPS * g + i)] for i in range(GROUPS)], 0)


def slot_rows(packets, piece, lanes):
    return jnp.concatenate([p[:piece, lanes] for p in packets], 0)


def attention_kernel(chips, line, *refs):
    query, packets, rows, seg, gain, near, far, *rest = take(
        refs, None, line, None, None, None, chips, chips, *[None] * 7
    )
    probs, attn, mid, hidden, bias, att3, acc4 = rest
    s = lax.axis_index("seq")
    piece = rows.shape[1]
    mine = jnp.broadcast_to(seg[...].astype(F32), (piece, piece)).T
    at = lax.broadcasted_iota(jnp.int32, (piece, piece), 0)
    key = lax.broadcasted_iota(jnp.int32, (piece, piece), 1)
    for k in range(line):
        same = mine == packets[k][piece : piece + 1, :piece].astype(F32)
        ok = same & (key - k * piece <= at) & (key + (s - k) * piece >= 0)
        bias[:, k * piece : (k + 1) * piece] = jnp.where(ok, 0.0, -jnp.inf)
    for g in range(KV_HEADS):
        keys = slot_rows(packets, piece, head_of(g))
        values = slot_rows(packets, piece, head_of(KV_HEADS + g))
        scores = right_mmul(group_rows(query, g), keys) * INV_ROOT
        scores = scores + jnp.concatenate([bias[...]] * GROUPS, 0)
        raised = jnp.exp(scores - jnp.max(scores, -1, keepdims=True))
        weights = raised / jnp.sum(raised, -1, keepdims=True)
        probs[g] = weights
        out = mmul(weights.astype(BF), values).astype(BF)
        for i in range(GROUPS):
            attn[:, head_of(GROUPS * g + i)] = out[i * piece : (i + 1) * piece]
    split_lanes(att3, attn[...], att3.shape[0])

    def body(k, carry):
        acc = 0.0
        for ref, _, m, j in blocks(near, far):
            acc = acc + mmul(att3[j], ref[k, 1])
        acc4[s ^ k] = acc
        return carry

    lax.fori_loop(0, line, body, 0)
    x = rows[...].T + join_lanes(acc4, line)
    mid[...] = x
    hidden[...] = (x * rms_scale(x) * gain[...]).astype(BF)


def load_all(refs, scratch):
    rows = refs[0].shape[0]
    for i, ref in enumerate(refs):
        scratch[i * rows : (i + 1) * rows] = ref[...]


def load_slots(own, right, left, slots):
    s = lax.axis_index("seq")
    line = slots.shape[0]
    pltpu.sync_copy(own, slots.at[s])
    for far in range(1, line):

        @pl.when(s >= far)
        def _():
            pltpu.sync_copy(right[far - 1], slots.at[s - far])

        @pl.when(s + far < line)
        def _():
            pltpu.sync_copy(left[far - 1], slots.at[s + far])


def feed_kernel(chips, line, tile, *refs):
    hid, low, own, right, left, back_near, back_far, gate_s, up_s, inner_s, *scratch = take(
        refs, 2 * chips, 2 * chips, None, line - 1, line - 1, None, chips, *[None] * 11
    )
    slots, gate_w, up_w, down_w, hid_s, low_s, far_s, far_sems = scratch
    load_slots(own, right, left, slots)
    load_all(hid, hid_s)
    load_all(low, low_s)
    piece = hid[0].shape[0]
    units = own.shape[0] // 3
    for k in range(line):
        span = slice(k * units, (k + 1) * units)
        gate_w[span] = slots[k, :units]
        up_w[span] = slots[k, units : 2 * units]
        down_w[span] = slots[k, 2 * units :]
    half = chips * piece

    def run(back, base):
        def body(i, carry):
            span = pl.ds(pl.multiple_of(i * tile, tile), tile)
            read = pl.ds(pl.multiple_of(base + i * tile, tile), tile)
            h = hid_s[read]
            gate = right_mmul(h, gate_w[...])
            up = right_mmul(h, up_w[...])
            inner_grad = right_mmul(low_s[read], down_w[...])
            sigma = jax.nn.sigmoid(gate)
            inner_s[read] = (gate * sigma * up).astype(BF)
            grad_up = (inner_grad * gate * sigma).astype(BF)
            grad_gate = (inner_grad * up * sigma * (1.0 + gate * (1.0 - sigma))).astype(BF)
            gate_s[read] = grad_gate
            up_s[read] = grad_up
            total_back = mmul(grad_gate, gate_w[...]) + mmul(grad_up, up_w[...])
            back[span] = total_back.astype(BF)
            return carry

        lax.fori_loop(0, half // tile, body, 0)

    run(far_s, half)
    sends = [
        pltpu.make_async_copy(far_s.at[pl.ds(m * piece, piece)], back_far[m], far_sems.at[m])
        for m in range(chips)
    ]
    for send in sends:
        send.start()
    run(back_near, 0)
    for send in sends:
        send.wait()


def feed_grad_kernel(chips, line, *refs):
    hid, low, own, right, left, gate_s, up_s, inner_s, down_near, down_far, *rest = take(
        refs,
        *(2 * chips, 2 * chips, None, line - 1, line - 1, None, None, None, None, chips),
        *(None, line - 1, line - 1, *[None] * 5),
    )
    mine, to_left, to_right, slots, down_w, hid_s, low_s, terms = rest
    s = lax.axis_index("seq")
    load_slots(own, right, left, slots)
    load_all(hid, hid_s)
    load_all(low, low_s)
    piece = hid[0].shape[0]
    units = own.shape[0] // 3
    for k in range(line):
        down_w[k * units : (k + 1) * units] = slots[k, 2 * units :]
    half = chips * piece
    for m in range(chips):
        span = slice(m * piece, (m + 1) * piece)
        far = slice(half + m * piece, half + (m + 1) * piece)
        down_near[span] = mmul(inner_s[span], down_w[...]).astype(BF)
        down_far[m][...] = mmul(inner_s[far], down_w[...]).astype(BF)
    for n, (a, b) in enumerate(((gate_s, hid_s), (up_s, hid_s), (inner_s, low_s))):
        term = left_mmul(a[...], b[...])
        for k in range(line):
            terms[k, n * units : (n + 1) * units] = term[k * units : (k + 1) * units]
    mine[...] = terms[s]
    for k in range(1, line):
        for out, ok, at in (
            (to_left[k - 1], s >= k, s - k),
            (to_right[k - 1], s + k < line, s + k),
        ):

            @pl.when(ok)
            def _():
                out[...] = terms[at].astype(BF)

            @pl.when(jnp.logical_not(ok))
            def _():
                out[...] = jnp.zeros(out.shape, BF)


def add_kernel(*refs):
    count = len(refs) // 3
    for i in range(count):
        a, b, out = refs[2 * i], refs[2 * i + 1], refs[2 * count + i]
        out[...] = (a[...].astype(F32) + b[...].astype(F32)).astype(BF)


def middle_kernel(chips, line, *refs):
    parts, mid, out_grad, gain, attn, query, probs, cosine, sine, near, far, packets, *rest = take(
        refs, chips, *[None] * 8, chips, chips, line, *[None] * 4, line, *[None] * 4
    )
    grad_mid, gain_term, grad_low, grad_query, slots, low4, att3, grad_attn, grad_kv = rest
    s = lax.axis_index("seq")
    piece = mid.shape[0]
    cos, sin = tables(cosine, sine)
    grad = parts[0][...].astype(F32)
    for part in parts[1:]:
        grad = grad + part[...].astype(F32)
    x = mid[...]
    scale = rms_scale(x)
    back, term = norm_back(grad, x * scale, scale, gain[...])
    gain_term[...] = term
    whole = out_grad[...].T + back
    grad_mid[...] = whole
    low = whole.astype(BF)
    grad_low[...] = low
    split_lanes(low4, low, line)
    for ref, _, m, j in blocks(near, far):
        acc = 0.0
        for k in range(line):
            acc = acc + right_mmul(low4[s ^ k], ref[k, 1])
        att3[j] = acc.astype(BF)
    grad_attn[...] = join_lanes(att3, att3.shape[0])
    for g in range(KV_HEADS):
        keys = slot_rows(packets, piece, head_of(g))
        values = slot_rows(packets, piece, head_of(KV_HEADS + g))
        q = group_rows(query, g)
        ga = group_rows(grad_attn, g)
        at = group_rows(attn, g)
        dots = jnp.sum(ga.astype(F32) * at.astype(F32), -1, keepdims=True)
        weights = probs[g]
        gs = (weights * (right_mmul(ga, values) - dots) * INV_ROOT).astype(BF)
        gq = mmul(gs, keys)
        for i in range(GROUPS):
            u = gq[i * piece : (i + 1) * piece]
            h = GROUPS * g + i
            grad_query[:, head_of(h)] = (u * cos - swapped(u) * sin).astype(BF)
        grad_kv[:, head_of(g)] = left_mmul(gs, q)
        grad_kv[:, head_of(KV_HEADS + g)] = left_mmul(weights.astype(BF), ga)
    for k in range(line):
        slots[k][...] = grad_kv[k * piece : (k + 1) * piece].astype(slots[k].dtype)


def query_grad_kernel(chips, *refs):
    hidden, grad_query, attn, grad_low, near, far, out_near, out_far, back, *scratch = take(
        refs, *[None] * 4, chips, chips, chips, chips, *[None] * 5
    )
    hid3, att3, gq4, low4 = scratch
    line = near[0].shape[0]
    s = lax.axis_index("seq")
    size = hid3.shape[0]
    split_lanes(hid3, hidden[...], size)
    split_lanes(att3, attn[...], size)
    split_lanes(gq4, grad_query[...], line)
    split_lanes(low4, grad_low[...], line)

    def body(k, carry):
        for ref, core, m, j in blocks(near, far):
            out = (out_near, out_far)[core][m]
            out[k, 0] = left_mmul(hid3[j], gq4[s ^ k]).astype(BF)
            out[k, 1] = left_mmul(att3[j], low4[s ^ k]).astype(BF)
        return carry

    lax.fori_loop(0, line, body, 0)
    for ref, _, m, j in blocks(near, far):
        acc = 0.0
        for k in range(line):
            acc = acc + right_mmul(gq4[s ^ k], ref[k, 0])
        back[j] = acc


def input_grad_kernel(chips, line, *refs):
    parts, rows, gain, hidden, grad_mid, base, cosine, sine, feed_term, near, far, *rest = take(
        refs, line, *[None] * 8, chips, chips, None, 2 * chips, *[None] * 4
    )
    result, outs, hid3, full, gkv4, x3 = take(rest, *[None] * 6)
    cos, sin = tables(cosine, sine)
    s = lax.axis_index("seq")
    size = hid3.shape[0]
    both = parts[0][...]
    for part in parts[1:]:
        both = both + part[...].astype(F32)
    for h in range(KV_HEADS):
        u = both[:, head_of(h)]
        full[:, head_of(h)] = (u * cos - swapped(u) * sin).astype(BF)
    full[:, KV_WIDTH:] = both[:, KV_WIDTH:].astype(BF)
    wide = KV_WIDTH // line
    for p in range(line):
        gkv4[p, :, :wide] = full[:, p * wide : (p + 1) * wide]
        gkv4[p, :, wide:] = full[:, KV_WIDTH + p * wide : KV_WIDTH + (p + 1) * wide]
    split_lanes(hid3, hidden[...], size)
    for ref, _, m, j in blocks(near, far):
        acc = base[j]
        for k in range(line):
            acc = acc + right_mmul(gkv4[s ^ k], ref[k])
        x3[j] = acc
    x = rows[...].T
    scale = rms_scale(x)
    back, term = norm_back(join_lanes(x3, size), x * scale, scale, gain[...])
    result[...] = (grad_mid[...] + back).T
    rows_of = hid3.shape[2]
    lanes = 2 * wide
    each = x.shape[1] // lanes
    for ref, core, m, j in blocks(near, far):
        out = outs[core * chips + m]
        for k in range(line):
            span = slice(k * rows_of, (k + 1) * rows_of)
            out[span] = left_mmul(hid3[j], gkv4[s ^ k]).astype(BF)
        base_row = line * rows_of
        out[base_row:] = jnp.zeros((out.shape[0] - base_row, lanes), BF)
        for n, value in enumerate((term, feed_term[...])):
            for i in range(each):
                at = base_row + n * each + i
                out[at : at + 1] = value[:, i * lanes : (i + 1) * lanes].astype(BF)


def join_kernel(key, value, query, output, out):
    a = key.shape[0]
    b = query.shape[1]
    out[:, :a] = key[...].T
    out[:, a : 2 * a] = value[...].T
    out[:, 2 * a : 2 * a + b] = query[...]
    out[:, 2 * a + b :] = output[...]


def stack_kernel(line, *refs):
    slots, kv, qo = take(refs, line, None, None)
    a = kv.shape[2]
    b = qo.shape[3]
    for k in range(line):
        kv[k] = slots[k][:, :a]
        qo[k, 0] = slots[k][:, a : a + b]
        qo[k, 1] = slots[k][:, a + b :]


def cast_kernel(grad, out):
    out[...] = grad[...].T.astype(BF)


def spread_kernel(gate, up, down, out):
    units = out.shape[2]
    for j in range(out.shape[0]):
        span = slice(j * units, (j + 1) * units)
        out[j, 0] = gate[:, span].T
        out[j, 1] = up[:, span].T
        out[j, 2] = down[:, span].T


def arrange_kernel(got, out):
    cut = got.shape[3]
    units = got.shape[2]
    for j in range(got.shape[0]):
        for n in range(3):
            out[n * units : (n + 1) * units, j * cut : (j + 1) * cut] = got[j, n]


def pair_sum_kernel(chips, *refs):
    near, got, own, outs = take(refs, chips, chips, None, chips - 1)
    own[...] = near[0][...].astype(F32) + got[0][...].astype(F32)
    for m in range(1, chips):
        outs[m - 1][...] = (near[m][...].astype(F32) + got[m][...].astype(F32)).astype(BF)


def stack_sum_kernel(chips, near, *refs):
    got, own, outs = take(refs, chips, None, chips - 1)
    rows = own.shape[0]
    own[...] = near[:rows].astype(F32) + got[0][...].astype(F32)
    for m in range(1, chips):
        mine = near[m * rows : (m + 1) * rows].astype(F32)
        outs[m - 1][...] = (mine + got[m][...].astype(F32)).astype(BF)


def down_end_kernel(mid, own, *refs):
    *got, out = refs
    out[...] = (mid[...] + tree([own[...]] + [g[...].astype(F32) for g in got])).T


def feed_end_kernel(own, *refs):
    left, right, out = refs
    whole = own[...] + left[...].astype(F32) + right[...].astype(F32)
    split_lanes(out, whole.astype(BF), out.shape[0])


def feed_done_kernel(got, gate, up, down):
    units = got.shape[2]
    for j in range(got.shape[0]):
        span = slice(j * units, (j + 1) * units)
        gate[:, span] = got[j, 0].astype(F32).T
        up[:, span] = got[j, 1].astype(F32).T
        down[:, span] = got[j, 2].astype(F32).T


def qo_line_kernel(chips, own, *refs):
    got, mine, sent = take(refs, chips - 1, None, len(refs) - chips)
    for k in range(own.shape[0]):
        whole = tree([own[k]] + [g[k].astype(F32) for g in got])
        if k == 0:
            mine[...] = whole
        else:
            sent[k - 1][...] = whole.astype(BF)


def qo_end_kernel(own, *refs):
    *got, query, output = refs
    query[...] = tree([own[0]] + [g[0].astype(F32) for g in got])
    output[...] = tree([own[1]] + [g[1].astype(F32) for g in got])


def kv_line_kernel(chips, line, own, *refs):
    got, mine, gains, sent = take(refs, chips - 1, None, None, line - 1)
    cut = mine.shape[0]
    last = slice(line * cut, None)
    term = tree([own[last].astype(BF).astype(F32)] + [g[last].astype(F32) for g in got]).astype(BF)
    gains[...] = term.astype(F32)
    for k in range(line):
        span = slice(k * cut, (k + 1) * cut)
        whole = tree([own[span]] + [g[span].astype(F32) for g in got])
        if k == 0:
            mine[...] = whole
        else:
            sent[k - 1][:cut] = whole.astype(BF)
            sent[k - 1][cut:] = term


def kv_end_kernel(line, own, own_gains, *refs):
    got, keys, values, attn_gain, feed_gain = take(refs, line - 1, *[None] * 4)
    cut, lanes = own.shape
    whole = tree([own[...]] + [g[:cut].astype(F32) for g in got])
    keys[...] = whole[:, : lanes // 2].T
    values[...] = whole[:, lanes // 2 :].T
    gains = tree([own_gains[...]] + [g[cut:].astype(F32) for g in got])
    each = attn_gain.shape[1] // lanes
    for n, out in enumerate((attn_gain, feed_gain)):
        for i in range(each):
            out[:, i * lanes : (i + 1) * lanes] = gains[n * each + i : n * each + i + 1]


def padded(a):
    if len(a.shape) < 2:
        return 4096
    size = jnp.dtype(a.dtype).itemsize
    *outer, rows, lanes = a.shape
    tile = 32 // size
    return math.prod(outer) * (-(-rows // tile) * tile) * (-(-lanes // 128) * 128) * size


def call(kernel, outs, scratch, flops, *args, far=(), far_outs=(), grant=True):
    sizes = [a.size * a.dtype.itemsize for a in (*args, *outs)]
    vmem = pl.BlockSpec(memory_space=pltpu.VMEM)
    free = pl.BlockSpec(memory_space=pl.ANY)
    held = [a for i, a in enumerate(args) if i not in far]
    held += [a for i, a in enumerate(outs) if i not in far_outs]
    held += [array(*x) for x in scratch if isinstance(x, tuple)]
    limit = min(sum(padded(a) for a in held) + ROOM * 2**20, 60 * 1024 * 2**10) if grant else None
    return pl.pallas_call(
        kernel,
        out_shape=outs,
        in_specs=[free if i in far else vmem for i in range(len(args))],
        out_specs=[free if i in far_outs else vmem for i in range(len(outs))],
        scratch_shapes=[x if not isinstance(x, tuple) else pltpu.VMEM(x[0], x[1]) for x in scratch],
        cost_estimate=pl.CostEstimate(
            flops=int(flops), bytes_accessed=sum(sizes), transcendentals=0
        ),
        compiler_params=pltpu.CompilerParams(vmem_limit_bytes=limit),
    )(*args)


def array(shape, dtype):
    return jax.ShapeDtypeStruct(shape, dtype)


def flip(x, bits):
    n = lax.axis_size("batch")
    return lax.ppermute(x, "batch", [(i, i ^ bits) for i in range(n)])


def cross(x, bits):
    n = lax.axis_size("seq")
    return lax.ppermute(x, "seq", [(i, i ^ bits) for i in range(n)])


def push(x, by):
    n = lax.axis_size("seq")
    pairs = [(i, i + by) for i in range(n) if 0 <= i + by < n]
    return lax.ppermute(x, "seq", pairs)


def tree(terms):
    while len(terms) > 1:
        terms = [terms[i] + terms[i + 1] for i in range(0, len(terms), 2)]
    return terms[0]


def plane_hops(x, chips):
    return [x] + [flip(x, 2 * m) for m in range(1, chips)]


def pair_swap(xs):
    return [flip(x, 1) for x in xs]


def plane_sum(near, far, chips):
    got = pair_swap(far)
    block = far[0].shape
    one = not isinstance(near, (list, tuple))
    own, *low = call(
        functools.partial(stack_sum_kernel if one else pair_sum_kernel, chips),
        [array(block, F32)] + [array(block, BF)] * (chips - 1),
        [],
        1e6,
        *([near] if one else near),
        *got,
    )
    return own, [flip(low[m - 1], 2 * m) for m in range(1, chips)]


def line_chain(x, line):
    out = []
    for by in (1, -1):
        held = x
        got = []
        for k in range(1, line):
            held = step(held, by, k)
            got.append(held)
        out.append(got)
    return out


def hand(x, by, k):
    n = lax.axis_size("seq")
    senders = range(n - k) if by > 0 else range(k, n)
    return lax.ppermute(x, "seq", [(i, i + by) for i in senders])


def step(x, by, k):
    n = lax.axis_size("seq")
    senders = range(k - 1, n - 1) if by > 0 else range(1, n - k + 1)
    return lax.ppermute(x, "seq", [(i, i + by) for i in senders])


def shards(
    activations,
    segment_ids,
    attention_gain,
    query_weight,
    key_weight,
    value_weight,
    output_weight,
    feed_gain,
    gate_weight,
    up_weight,
    down_weight,
    out_grad,
):
    piece, width = activations.shape[1:]
    line = lax.axis_size("seq")
    size = lax.axis_size("batch")
    length = piece * line
    chips = size // 2
    cut = width // size
    rows = activations[0].T
    grad_rows = out_grad[0].T
    s = lax.axis_index("seq")
    positions = s * piece + jnp.arange(piece, dtype=jnp.int32)
    cosine, sine = rotary_tables(positions.astype(F32))
    gain_attn = attention_gain[None]
    gain_feed = feed_gain[None]
    units = gate_weight.shape[1] // size
    others = range(1, line)

    kv_cols = 2 * key_weight.shape[1]
    qo_cols = query_weight.shape[1]
    (own,) = call(
        join_kernel,
        [array((cut, kv_cols + 2 * qo_cols), BF)],
        [],
        1e5,
        key_weight.T,
        value_weight.T,
        query_weight,
        output_weight,
        grant=False,
    )
    kv_slots, qo_slots = call(
        functools.partial(stack_kernel, line),
        [array((line, cut, kv_cols), BF), array((line, 2, cut, qo_cols), BF)],
        [],
        1e5,
        own,
        *[cross(own, k) for k in others],
    )
    kv_near = plane_hops(kv_slots, chips)
    kv_far = pair_swap(kv_near)
    qo_near = plane_hops(qo_slots, chips)
    qo_far = pair_swap(qo_near)

    (local,) = call(
        spread_kernel,
        [array((size, 3, units, cut), BF)],
        [],
        1e5,
        gate_weight,
        up_weight,
        down_weight.T,
        grant=False,
    )
    spread = lax.all_to_all(local, "batch", split_axis=0, concat_axis=0, tiled=True)
    (feed_own,) = call(arrange_kernel, [array((3 * units, width), BF)], [], 1e5, spread)
    feed_right, feed_left = line_chain(feed_own, line)

    (low,) = call(cast_kernel, [array((piece, width), BF)], [], 1e5, grad_rows, grant=False)
    low_near = plane_hops(low, chips)
    low_far = pair_swap(low_near)

    hidden_attn, packet = call(
        functools.partial(kv_kernel, chips),
        [array((piece, width), BF), array((piece + 8, 2 * KV_WIDTH), BF)],
        [((size, piece, cut), BF), ((line, piece, kv_cols), F32)],
        2 * piece * width * 2 * KV_WIDTH,
        rows,
        gain_attn,
        cosine,
        sine,
        segment_ids,
        *kv_near,
        *kv_far,
    )
    packets = [packet] + [push(packet, k) for k in others]
    (query,) = call(
        functools.partial(query_kernel, chips),
        [array((piece, width), BF)],
        [((size, piece, cut), BF), ((line, piece, qo_cols), F32)],
        2 * piece * width * width,
        hidden_attn,
        cosine,
        sine,
        *qo_near,
        *qo_far,
    )
    probs, attn, mid, hidden_feed = call(
        functools.partial(attention_kernel, chips, line),
        [
            array((KV_HEADS, GROUPS * piece, length), F32),
            array((piece, width), BF),
            array((piece, width), F32),
            array((piece, width), BF),
        ],
        [((piece, length), F32), ((size, piece, cut), BF), ((line, piece, qo_cols), F32)],
        2 * piece * width * (width + 2 * length),
        query,
        *packets,
        rows,
        segment_ids,
        gain_feed,
        *qo_near,
        *qo_far,
    )
    hid_near = plane_hops(hidden_feed, chips)
    hid_far = pair_swap(hid_near)
    flat = (chips * piece, width)
    tokens = size * piece
    act = (tokens, line * units)
    feed_in = [*hid_near, *hid_far, *low_near, *low_far, feed_own, *feed_right, *feed_left]
    slots = [((line, 3 * units, width), BF), ((line * units, width), BF)]
    both = [((tokens, width), BF)] * 2
    kept = range(4 * chips, len(feed_in))
    back_near, *rest = call(
        functools.partial(feed_kernel, chips, line, 2 * piece),
        [array(flat, BF)] + [array((piece, width), BF)] * chips + [array(act, BF)] * 3,
        [
            slots[0],
            slots[1],
            slots[1],
            slots[1],
            *both,
            (flat, BF),
            pltpu.SemaphoreType.DMA((chips,)),
        ],
        10 * tokens * width * line * units,
        *feed_in,
        far=kept,
        far_outs=range(1, chips + 1),
    )
    back_far, acts = rest[:chips], rest[chips:]
    back_own, back_got = plane_sum(back_near, back_far, chips)
    down_near, *rest = call(
        functools.partial(feed_grad_kernel, chips, line),
        [array(flat, BF)]
        + [array((piece, width), BF)] * chips
        + [array((3 * units, width), F32)]
        + [array((3 * units, width), BF)] * (2 * line - 2),
        [*slots, *both, ((line, 3 * units, width), F32)],
        8 * tokens * width * line * units,
        *feed_in,
        *acts,
        far=kept,
    )
    down_far, feed_grads = rest[:chips], rest[chips:]
    grad_mid, feed_term, grad_mid_low, grad_query, kv_own, *kv_sent = call(
        functools.partial(middle_kernel, chips, line),
        [
            array((piece, width), F32),
            array((1, width), F32),
            array((piece, width), BF),
            array((piece, width), BF),
            array((piece, 2 * KV_WIDTH), F32),
        ]
        + [array((piece, 2 * KV_WIDTH), BF)] * (line - 1),
        [
            ((line, piece, qo_cols), BF),
            ((size, piece, cut), BF),
            ((piece, width), BF),
            ((length, 2 * KV_WIDTH), F32),
        ],
        2 * piece * width * (width + 4 * length),
        back_own,
        *back_got,
        mid,
        grad_rows,
        gain_feed,
        attn,
        query,
        probs,
        cosine,
        sine,
        *qo_near,
        *qo_far,
        *packets,
    )
    kv_got = [push(kv_sent[k - 1], -k) for k in others]

    down_own, down_got = plane_sum(down_near, down_far, chips)
    (block_output,) = call(
        down_end_kernel, [array((width, piece), F32)], [], 1e6, mid, down_own, *down_got
    )

    to_left, to_right = feed_grads[1:line], feed_grads[line:]
    left, right = to_left[-1], to_right[-1]
    for k in range(line - 1, 0, -1):
        left = hand(left, -1, k)
        right = hand(right, 1, k)
        if k > 1:
            left, right = call(
                add_kernel,
                [array(left.shape, BF)] * 2,
                [],
                1e6,
                left,
                to_left[k - 2],
                right,
                to_right[k - 2],
            )
    (feed_own,) = call(
        feed_end_kernel, [array((size, 3 * units, cut), BF)], [], 1e6, feed_grads[0], left, right
    )
    feed_back = lax.all_to_all(feed_own, "batch", split_axis=0, concat_axis=0, tiled=True)
    gate_done, up_done, down_done = call(
        feed_done_kernel,
        [
            array(gate_weight.shape, F32),
            array(up_weight.shape, F32),
            array(down_weight.shape[::-1], F32),
        ],
        [],
        1e6,
        feed_back.reshape(size, 3, units, cut),
    )

    shape = (line, 2, cut, qo_cols)
    *qo_grads, base = call(
        functools.partial(query_grad_kernel, chips),
        [array(shape, BF)] * size + [array((size, piece, cut), F32)],
        [((size, piece, cut), BF)] * 2 + [((line, piece, qo_cols), BF)] * 2,
        6 * piece * width * width,
        hidden_attn,
        grad_query,
        attn,
        grad_mid_low,
        *qo_near,
        *qo_far,
    )
    qo_own, qo_got = plane_sum(qo_grads[:chips], qo_grads[chips:], chips)
    block = (2, cut, qo_cols)
    qo_own, *qo_sent = call(
        functools.partial(qo_line_kernel, chips),
        [array(block, F32)] + [array(block, BF)] * (line - 1),
        [],
        1e6,
        qo_own,
        *qo_got,
    )
    qo_got = [cross(qo_sent[k - 1], k) for k in others]
    query_done, output_done = call(
        qo_end_kernel, [array((cut, qo_cols), F32)] * 2, [], 1e6, qo_own, *qo_got
    )

    each = width // kv_cols
    extra = -(-2 * each // 16) * 16
    shape = (line * cut + extra, kv_cols)
    input_grad, *kv_grads = call(
        functools.partial(input_grad_kernel, chips, line),
        [array((width, piece), F32)] + [array(shape, BF)] * size,
        [
            ((size, piece, cut), BF),
            ((piece, 2 * KV_WIDTH), BF),
            ((line, piece, kv_cols), BF),
            ((size, piece, cut), F32),
        ],
        4 * piece * width * 2 * KV_WIDTH,
        kv_own,
        *kv_got,
        rows,
        gain_attn,
        hidden_attn,
        grad_mid,
        base,
        cosine,
        sine,
        feed_term,
        *kv_near,
        *kv_far,
    )
    kv_own, kv_got = plane_sum(kv_grads[:chips], kv_grads[chips:], chips)
    kv_own, own_gains, *kv_sent = call(
        functools.partial(kv_line_kernel, chips, line),
        [array((cut, kv_cols), F32), array((extra, kv_cols), F32)]
        + [array((cut + extra, kv_cols), BF)] * (line - 1),
        [],
        1e6,
        kv_own,
        *kv_got,
    )
    kv_got = [cross(kv_sent[k - 1], k) for k in others]
    key_done, value_done, attn_gain_sum, feed_gain_sum = call(
        functools.partial(kv_end_kernel, line),
        [array((kv_cols // 2, cut), F32)] * 2 + [array((1, width), F32)] * 2,
        [],
        1e6,
        kv_own,
        own_gains,
        *kv_got,
    )
    return (
        block_output.T[None],
        input_grad.T[None],
        attn_gain_sum[0],
        query_done,
        key_done.T,
        value_done.T,
        output_done,
        feed_gain_sum[0],
        gate_done,
        up_done,
        down_done.T,
    )


def solution(mesh):
    both = P("batch", "seq")
    tokens = P("batch", "seq", None)
    in_specs = (tokens, both, P(), both, both, both, both, P(), both, both, P("seq", "batch"), tokens)
    out_specs = (tokens, tokens, P(), both, both, both, both, P(), both, both, P("seq", "batch"))

    return jax.shard_map(shards, mesh=mesh, in_specs=in_specs, out_specs=out_specs, check_vma=False)
```
